256 devices in a mesh: dp: 4 (over z_hi), ctx: 16 (over y, z_lo, core), tp: 4 (over x).
Axes of the slice: x: 4, y: 4, z: 8 (z_hi: 4, z_lo: 2; z = z_hi * 2 + z_lo), core: 2. Of those that a mesh axis runs over, the one named last changes fastest.
Arguments:
- queries: bfloat16 [12288, 4096], P(('dp', 'ctx'), 'tp'), parts along dimension 0, may hold values from -40 to 40
- keys: bfloat16 [12288, 512], P(('dp', 'ctx'), 'tp'), parts along dimension 0, may hold values from -4 to 4
- values: bfloat16 [12288, 512], P(('dp', 'ctx'), 'tp'), parts along dimension 0, may hold values from -6 to 6
- grad_out: bfloat16 [12288, 4096], P(('dp', 'ctx'), 'tp'), parts along dimension 0, may hold values from -6 to 6
- segments: int32 [12288], P(('dp', 'ctx')), parts along dimension 0, may hold values from 0 to 5, never falling along the last dimension, each value on 1 to 2304 neighbouring positions
- sinks: float32 [64], P('tp'), may hold values from -1 to 5
Outputs:
- grad_queries: bfloat16 [12288, 4096], P(('dp', 'ctx'), 'tp'), parts along dimension 0
- keys_gradient: bfloat16 [12288, 512], P(('dp', 'ctx'), 'tp'), parts along dimension 0
- values_gradient: bfloat16 [12288, 512], P(('dp', 'ctx'), 'tp'), parts along dimension 0
- grad_sinks: float32 [256], P(('dp', 'tp')), parts along dimension 0
The draws below stay inside these ranges and needn't reach their ends.
There are 4 independent parts, one for each index of `dp`. The reference program is written for one: setup_inputs(seed, part) draws one part's arguments, and reference() takes and returns one part's arrays. A program takes and returns all parts, laid end to end along the dimension named above; an argument that names none is the same for every part. Nothing has to cross between parts.
All inputs are finite; a program needn't handle non-finite values.
Results may differ from the reference program's by a relative error of at most 0.012.
The reference program's roundings to bfloat16 on the way (of `prob_half` and `dscore`) count: a program that leaves them out, or rounds other values in their place, can miss the bound.
Values may be sent and summed in bfloat16 or wider, within the bound.
A program may use at most 64 MiB of HBM per device.

```python
import math
import jax
import jax.numpy as jnp
import numpy as np
from jax import lax

QUERY_HEAD_COUNT = 64
KEY_VALUE_HEADS = 8
HEAD_SIZE = 64
DOCS = 6
SEQUENCE_TOKENS = 3072


def draw_keys(key, part):
    drawn_result = jax.random.truncated_normal(jax.random.fold_in(key, 11), -4.0, 4.0, (SEQUENCE_TOKENS, KEY_VALUE_HEADS * HEAD_SIZE)).astype(jnp.float32)
    return drawn_result.astype(jnp.bfloat16)


def draw_queries(key, part):
    drawn_result = jax.random.truncated_normal(jax.random.fold_in(key, 12), -4.0, 4.0, (SEQUENCE_TOKENS, QUERY_HEAD_COUNT * HEAD_SIZE)).astype(jnp.float32)
    return drawn_result.astype(jnp.bfloat16)


def block_levels(rng, extent, pieces, least, largest):
    factor_of = 1.0
    for dim, parts in pieces:
        draws = jax.random.uniform(jax.random.fold_in(jax.random.fold_in(rng, 6), dim), (parts,), jnp.float32, least / len(pieces), largest / len(pieces))
        factor_of = factor_of * jnp.repeat(jnp.exp(draws), extent[dim] // parts).reshape((-1,) + (1,) * (len(extent) - 1 - dim))
    return factor_of


def length_profile(count, total, limit, lean):
    portions = [(1 << 20) // math.isqrt(rank ** lean) + 1 for rank in range(2, count + 1)]
    surplus, holding = total - limit - (count - 1), [1] * (count - 1)
    while surplus > 0:
        movable = [i for i in range(count - 1) if holding[i] < limit]
        pool, budget = sum([portions[i] for i in movable]), surplus
        for i in movable:
            addition = min(limit - holding[i], max(1, budget * portions[i] // pool), surplus)
            holding[i] = holding[i] + addition
            surplus = surplus - addition
    return np.array([limit] + holding)


def uneven(key, count, total, most, skew):
    if count == 2:
        one = jax.random.randint(key, (), max(1, total - most), min(most, total - 1) + 1)
        return jnp.stack([one, total - one])
    tallies = jnp.asarray(length_profile(count, total, most, skew), jnp.int32)
    twos = (count - 1) // 2
    donor, taker = tallies[1:1 + 2 * twos:2], tallies[2:2 + 2 * twos:2]
    slack = jnp.minimum(donor - 1, most - taker)
    passed = jax.random.randint(jax.random.fold_in(key, 1), (twos,), 0, 1 << 20) % (slack + 1)
    tallies = tallies.at[1:1 + 2 * twos:2].set(donor - passed).at[2:2 + 2 * twos:2].set(taker + passed)
    return tallies[jax.random.permutation(jax.random.fold_in(key, 2), count)]


def centred(stream_key, dims, width, reach, cuts=(), held_as=jnp.bfloat16):
    result = jax.random.normal(stream_key, dims, jnp.float32) * width
    if len(cuts) > 0:
        result = block_levels(stream_key, dims, cuts, -0.22, 0.18) * result
    return jnp.clip(result, min=-reach, max=reach).astype(held_as)


def setup_inputs(seed: int = 0, part: int = 0) -> dict:
    streams_of = jax.random.split(jax.random.key(seed), 7)
    own_keys = jax.random.split(jax.random.fold_in(streams_of[6], part), 7)
    queries = draw_queries(jax.random.fold_in(jax.random.fold_in(streams_of[6], part), 71), part)
    keys = draw_keys(jax.random.fold_in(jax.random.fold_in(streams_of[6], part), 71), part)
    values = centred(own_keys[2], (SEQUENCE_TOKENS, KEY_VALUE_HEADS * HEAD_SIZE), 1.0, 6.0, ((0, 16), (1, 4)))
    grad_out = centred(own_keys[3], (SEQUENCE_TOKENS, QUERY_HEAD_COUNT * HEAD_SIZE), 1.0, 6.0, ((0, 16), (1, 4)))
    segments = jnp.searchsorted(jnp.cumsum(uneven(own_keys[4], DOCS, SEQUENCE_TOKENS, 3 * SEQUENCE_TOKENS // 4, 0)), jnp.arange(SEQUENCE_TOKENS), side="right").astype(jnp.int32)
    sinks = jnp.clip(-1.0 + 6.0 * jax.random.uniform(streams_of[5], (QUERY_HEAD_COUNT,), jnp.float32) ** block_levels(streams_of[5], (QUERY_HEAD_COUNT,), ((0, 4),), -0.2, 0.2), -1.0, 5.0)
    return {"queries": queries, "keys": keys, "values": values, "grad_out": grad_out, "segments": segments, "sinks": sinks}


def reference(queries, keys, values, grad_out, segments, sinks):
    total_sum = queries.shape[0]
    query_group = QUERY_HEAD_COUNT // KEY_VALUE_HEADS
    scale = HEAD_SIZE ** -0.5
    position = jnp.arange(total_sum, dtype=jnp.int32)
    allowed = (position[None, :] <= position[:, None]) & (segments[None, :] == segments[:, None])

    def one_head(head):
        kv_index = head // query_group
        sink = sinks[head]
        query_head = lax.dynamic_slice_in_dim(queries, (head * HEAD_SIZE).astype(jnp.int32), HEAD_SIZE, 1)
        key_head = lax.dynamic_slice_in_dim(keys, (kv_index * HEAD_SIZE).astype(jnp.int32), HEAD_SIZE, 1)
        value_head = lax.dynamic_slice_in_dim(values, (kv_index * HEAD_SIZE).astype(jnp.int32), HEAD_SIZE, 1)
        grad_head = lax.dynamic_slice_in_dim(grad_out, (head * HEAD_SIZE).astype(jnp.int32), HEAD_SIZE, 1)
        raw = jnp.dot(query_head, key_head.T, preferred_element_type=jnp.float32) * scale
        masked = jnp.where(allowed, raw, -jnp.inf)
        top = jnp.maximum(jnp.max(masked, axis=1), sink)
        lse = top + jnp.log(jnp.exp(sink - top) + jnp.sum(jnp.exp(masked - top[:, None]), axis=1))
        prob = jnp.where(allowed, jnp.exp(raw - lse[:, None]), jnp.float32(0.0))
        prob_half = prob.astype(jnp.bfloat16)
        out = jnp.dot(prob_half, value_head, preferred_element_type=jnp.float32)
        delta = jnp.sum(grad_head.astype(jnp.float32) * out, axis=1)
        grad_sink = -jnp.sum(jnp.exp(sink - lse) * delta)
        dprob = jnp.dot(grad_head, value_head.T, preferred_element_type=jnp.float32)
        dscore = (prob * (dprob - delta[:, None])).astype(jnp.bfloat16)
        grad_query = jnp.dot(dscore, key_head, preferred_element_type=jnp.float32) * scale
        key_gradient = jnp.dot(dscore.T, query_head, preferred_element_type=jnp.float32) * scale
        value_gradient = jnp.dot(prob_half.T, grad_head, preferred_element_type=jnp.float32)
        return grad_query, key_gradient, value_gradient, grad_sink

    grad_query, key_gradient, value_gradient, grad_sinks = lax.map(one_head, jnp.arange(QUERY_HEAD_COUNT, dtype=jnp.int32))
    grad_queries = grad_query.transpose(1, 0, 2).reshape(total_sum, QUERY_HEAD_COUNT * HEAD_SIZE).astype(jnp.bfloat16)
    keys_gradient = key_gradient.reshape(KEY_VALUE_HEADS, query_group, total_sum, HEAD_SIZE).sum(axis=1)
    values_gradient = value_gradient.reshape(KEY_VALUE_HEADS, query_group, total_sum, HEAD_SIZE).sum(axis=1)
    keys_gradient = keys_gradient.transpose(1, 0, 2).reshape(total_sum, KEY_VALUE_HEADS * HEAD_SIZE).astype(jnp.bfloat16)
    values_gradient = values_gradient.transpose(1, 0, 2).reshape(total_sum, KEY_VALUE_HEADS * HEAD_SIZE).astype(jnp.bfloat16)
    return grad_queries, keys_gradient, values_gradient, grad_sinks
```

```python
import functools

import jax
import jax.numpy as jnp
from jax import lax
from jax.experimental import pallas as pl
from jax.experimental.pallas import tpu as pltpu
from jax.sharding import PartitionSpec as P

D = 64
PEERS = 16
ROWS = 192
HALF = 96
DOCS = 6
TILE = 128
LANES = 2 * TILE
CHUNK = 256
LOG2E = 1.4426950408889634
FILL = -1e30
f32 = jnp.float32
bf16 = jnp.bfloat16


def spot(i):
    return i // 4, lax.rem(i // 2, 2), lax.rem(i, 2)


def remote(src, dst, send, recv, to):
    return pltpu.make_async_remote_copy(
        src_ref=src,
        dst_ref=dst,
        send_sem=send,
        recv_sem=recv,
        device_id={"ctx": to},
        device_id_type=pl.DeviceIdType.MESH,
    )


def greet(me):
    barrier = pltpu.get_barrier_semaphore()

    def hello(i, c):
        to = lax.rem(me + i, PEERS)
        pl.semaphore_signal(
            barrier, inc=1, device_id={"ctx": to}, device_id_type=pl.DeviceIdType.MESH
        )
        return c

    lax.fori_loop(1, PEERS, hello, 0)
    pl.semaphore_wait(barrier, PEERS - 1)


def scatter_kernel(
    q_ref, g_ref, k_ref, v_ref, seg_ref,
    qo_ref, go_ref, kvo_ref, cnt_ref,
    kvbuf, cntbuf, cntall,
    qs, qr, gs, gr, ks, kr, fs, cs, cr, ls,
):
    me = lax.axis_index("ctx")
    y, z, c = spot(me)
    mate = me + 1 - 2 * c

    for h in range(2):
        kvbuf[h] = jnp.concatenate(
            [k_ref[:, h * D : (h + 1) * D], v_ref[:, h * D : (h + 1) * D]], axis=1
        )
    lane = lax.broadcasted_iota(jnp.int32, (1, 128), 1)
    row = jnp.zeros((1, 128), f32)
    for d in range(1, DOCS):
        below = jnp.sum(jnp.where(seg_ref[...] < d, 1.0, 0.0), axis=1, keepdims=True)
        row = jnp.where(lane == d, below, row)
    cntbuf[...] = row
    cntall[me] = row

    greet(me)

    def q_copy(to, frm):
        ty, tz, tc = spot(to)
        rows = pl.ds(pl.multiple_of(tc * HALF, 32), HALF)
        cols = pl.ds(pl.multiple_of(tz * 512 + ty * 128, 128), 128)
        land = pl.ds(pl.multiple_of(frm * HALF, 32), HALF)
        return (
            (q_ref.at[rows, cols], qo_ref.at[land], qs.at[to], qr.at[frm]),
            (g_ref.at[rows, cols], go_ref.at[land], gs.at[to], gr.at[frm]),
        )

    def kv_at(i):
        return kvo_ref.at[pl.ds(pl.multiple_of(i * ROWS, 64), ROWS)]

    (a, b) = q_copy(me, me)
    own_q = pltpu.make_async_copy(a[0], a[1], ls.at[0])
    own_g = pltpu.make_async_copy(b[0], b[1], ls.at[1])
    own_kv = pltpu.make_async_copy(kvbuf.at[z], kv_at(me), ls.at[2])
    own_q.start()
    own_g.start()
    own_kv.start()

    def kv_send(i, carry):
        to = lax.rem(me + 2 * i, PEERS)
        remote(kvbuf.at[spot(to)[1]], kv_at(me), ks.at[to], kr.at[me], to).start()
        return carry

    lax.fori_loop(1, 8, kv_send, 0)
    remote(kvbuf.at[z], kv_at(me), ks.at[mate], kr.at[me], mate).start()

    def cnt_send(i, carry):
        to = lax.rem(me + i, PEERS)
        remote(cntbuf, cntall.at[me], cs.at[to], cr.at[me], to).start()
        return carry

    lax.fori_loop(1, PEERS, cnt_send, 0)

    def q_send(i, carry):
        to = lax.rem(me + i, PEERS)
        for s in q_copy(to, me):
            remote(*s, to).start()
        return carry

    lax.fori_loop(1, PEERS, q_send, 0)

    def kv_pass(i, carry):
        frm = lax.rem(me + PEERS - 2 * i, PEERS)
        remote(kvbuf.at[0], kv_at(frm), ks.at[frm], kr.at[frm], frm).wait_recv()
        remote(kv_at(frm), kv_at(frm), fs.at[frm], kr.at[frm], mate).start()
        return carry

    lax.fori_loop(1, 8, kv_pass, 0)

    def kv_get(i, carry):
        frm = lax.rem(mate + 2 * i, PEERS)
        remote(kvbuf.at[0], kv_at(frm), ks.at[frm], kr.at[frm], frm).wait_recv()
        return carry

    lax.fori_loop(0, 8, kv_get, 0)

    def kv_sent(i, carry):
        to = lax.rem(me + 2 * i, PEERS)
        remote(kvbuf.at[0], kv_at(me), ks.at[to], kr.at[me], to).wait_send()
        remote(kv_at(to), kv_at(to), fs.at[to], kr.at[to], mate).wait_send()
        return carry

    lax.fori_loop(1, 8, kv_sent, 0)
    remote(kvbuf.at[0], kv_at(me), ks.at[mate], kr.at[me], mate).wait_send()

    def rest(i, carry):
        o = lax.rem(me + i, PEERS)
        for s in q_copy(o, o):
            cp = remote(*s, o)
            cp.wait_send()
            cp.wait_recv()
        cp = remote(cntbuf, cntall.at[o], cs.at[o], cr.at[o], o)
        cp.wait_send()
        cp.wait_recv()
        return carry

    lax.fori_loop(1, PEERS, rest, 0)
    own_q.wait()
    own_g.wait()
    own_kv.wait()
    total = cntall[0]
    for i in range(1, PEERS):
        total = total + cntall[i]
    cnt_ref[...] = total


def scatter(q, g, k, v, seg):
    any_ = pl.BlockSpec(memory_space=pl.ANY)
    vmem = pl.BlockSpec(memory_space=pltpu.VMEM)
    sem = pltpu.SemaphoreType.DMA
    total = PEERS * ROWS
    return pl.pallas_call(
        scatter_kernel,
        name="scatter",
        out_shape=(
            jax.ShapeDtypeStruct((total // 2, 128), bf16),
            jax.ShapeDtypeStruct((total // 2, 128), bf16),
            jax.ShapeDtypeStruct((total, 128), bf16),
            jax.ShapeDtypeStruct((1, 128), f32),
        ),
        in_specs=[any_, any_, vmem, vmem, vmem],
        out_specs=(any_, any_, any_, vmem),
        scratch_shapes=[
            pltpu.VMEM((2, ROWS, 128), bf16),
            pltpu.VMEM((1, 128), f32),
            pltpu.VMEM((PEERS, 1, 128), f32),
        ]
        + [sem((PEERS,))] * 9
        + [sem((3,))],
        compiler_params=pltpu.CompilerParams(collective_id=0, has_side_effects=True),
    )(q, g, k, v, seg)


def local_kernel(
    cnt_ref, sink_ref, q_ref, g_ref, kv_ref,
    dq_ref, dkv_ref, gs_ref,
    kt_ref, acc_ref, s_ref, dp_ref, gacc_ref,
):
    me = lax.axis_index("ctx")
    y, z, c = spot(me)
    total = kv_ref.shape[0]
    head = 8 * z + 2 * y
    begins = [cnt_ref[0, d].astype(jnp.int32) for d in range(1, DOCS)]

    acc_ref[...] = jnp.zeros_like(acc_ref)
    gacc_ref[...] = jnp.zeros_like(gacc_ref)

    def turn(j, carry):
        at = pl.multiple_of(j * CHUNK, CHUNK)
        both = kv_ref[pl.ds(at, CHUNK), :].astype(f32).T
        kt_ref[j] = both[:D].astype(bf16)
        return carry

    lax.fori_loop(0, total // CHUNK, turn, 0)

    lane = lax.broadcasted_iota(jnp.int32, (1, LANES), 1)
    sink = jnp.where(lane < TILE, sink_ref[head], sink_ref[head + 1])
    key_iota = lax.broadcasted_iota(jnp.int32, (CHUNK, LANES), 0)
    nt = (((1,), (1,)), ((), ()))

    def fold(x, op):
        return op(x.reshape(CHUNK // 8, 8, LANES), axis=0)

    def tile(t, carry):
        n0 = pl.multiple_of(t * TILE, TILE)
        s0 = n0 // HALF
        n = n0 + (lane & (TILE - 1))
        pos = n + HALF * (s0 + c) + jnp.where(n >= (s0 + 1) * HALF, HALF, 0)
        start = jnp.zeros_like(pos)
        p_first = n0 + HALF * (s0 + c)
        p_last = n0 + TILE - 1 + HALF * (s0 + 1 + c)
        first = 0
        for b in begins:
            start = jnp.where(pos >= b, b, start)
            first = jnp.where(p_first >= b, b, first)
        lo = first // CHUNK
        hi = p_last // CHUNK + 1

        qt = q_ref[pl.ds(n0, TILE), :]
        gt = g_ref[pl.ds(n0, TILE), :]
        qt = (qt.astype(f32) * 0.125).astype(bf16)
        none = jnp.zeros((TILE, D), bf16)
        wq = jnp.concatenate(
            [
                jnp.concatenate([qt[:, :D], none], axis=1),
                jnp.concatenate([qt[:, D:], none], axis=1),
            ],
            axis=0,
        )
        wg = jnp.concatenate(
            [
                jnp.concatenate([none, gt[:, :D]], axis=1),
                jnp.concatenate([none, gt[:, D:]], axis=1),
            ],
            axis=0,
        )
        w = jnp.concatenate([wq, wg], axis=0)

        def scores(j, top):
            kv = kv_ref[pl.ds(pl.multiple_of(j * CHUNK, CHUNK), CHUNK), :]
            at = pl.ds(pl.multiple_of((j - lo) * CHUNK, CHUNK), CHUNK)
            s = lax.dot_general(kv, wq, nt, preferred_element_type=f32)
            key = key_iota + j * CHUNK
            s = jnp.where((key >= start) & (key <= pos), s, FILL)
            s_ref[at, :] = s
            dp_ref[at, :] = lax.dot_general(kv, wg, nt, preferred_element_type=f32)
            return jnp.maximum(top, fold(s, jnp.max))

        top = lax.fori_loop(lo, hi, scores, jnp.full((8, LANES), FILL, f32))
        top = jnp.maximum(jnp.max(top, axis=0, keepdims=True), sink)

        def weights(j, mass):
            at = pl.ds(pl.multiple_of((j - lo) * CHUNK, CHUNK), CHUNK)
            e = jnp.exp2((s_ref[at, :] - top) * LOG2E)
            s_ref[at, :] = e
            return mass + fold(e, jnp.sum)

        mass = lax.fori_loop(lo, hi, weights, jnp.zeros((8, LANES), f32))
        sink_e = jnp.exp2((sink - top) * LOG2E)
        mass = jnp.sum(mass, axis=0, keepdims=True) + sink_e
        inv = 1.0 / mass

        def deltas(j, delta):
            at = pl.ds(pl.multiple_of((j - lo) * CHUNK, CHUNK), CHUNK)
            half = (s_ref[at, :] * inv).astype(bf16).astype(f32)
            return delta + fold(half * dp_ref[at, :], jnp.sum)

        delta = lax.fori_loop(lo, hi, deltas, jnp.zeros((8, LANES), f32))
        delta = jnp.sum(delta, axis=0, keepdims=True)
        gacc_ref[...] += sink_e * inv * delta

        def grads(j, dqt):
            at = pl.ds(pl.multiple_of((j - lo) * CHUNK, CHUNK), CHUNK)
            key = pl.ds(pl.multiple_of(j * CHUNK, CHUNK), CHUNK)
            prob = s_ref[at, :] * inv
            ds = (prob * (dp_ref[at, :] - delta)).astype(bf16)
            x = jnp.concatenate([ds, prob.astype(bf16)], axis=1)
            acc_ref[key, :] += jnp.dot(x, w, preferred_element_type=f32)
            return dqt + jnp.dot(kt_ref[j], ds, preferred_element_type=f32)

        dqt = lax.fori_loop(lo, hi, grads, jnp.zeros((D, LANES), f32))
        dq = (dqt * 0.125).T
        dq_ref[pl.ds(n0, TILE), :] = jnp.concatenate([dq[:TILE], dq[TILE:]], axis=1).astype(bf16)
        return carry

    lax.fori_loop(0, q_ref.shape[0] // TILE, tile, 0)
    dkv_ref[...] = acc_ref[...].astype(bf16)
    g = gacc_ref[...]
    ga = -jnp.sum(g[:, :TILE], axis=1, keepdims=True)
    gb = -jnp.sum(g[:, TILE:], axis=1, keepdims=True)
    l = lax.broadcasted_iota(jnp.int32, (1, 128), 1)
    gs_ref[...] = jnp.where(l == head, ga, jnp.where(l == head + 1, gb, 0.0))


def local(cnt, sinks, q, g, kv):
    vmem = pl.BlockSpec(memory_space=pltpu.VMEM)
    smem = pl.BlockSpec(memory_space=pltpu.SMEM)
    total = kv.shape[0]
    return pl.pallas_call(
        local_kernel,
        name="local",
        out_shape=(
            jax.ShapeDtypeStruct(q.shape, bf16),
            jax.ShapeDtypeStruct(kv.shape, bf16),
            jax.ShapeDtypeStruct((1, 128), f32),
        ),
        in_specs=[smem, smem, vmem, vmem, vmem],
        out_specs=(vmem, vmem, vmem),
        scratch_shapes=[
            pltpu.VMEM((total // CHUNK, D, CHUNK), bf16),
            pltpu.VMEM((total, 128), f32),
            pltpu.VMEM((total, LANES), f32),
            pltpu.VMEM((total, LANES), f32),
            pltpu.VMEM((1, LANES), f32),
        ],
        compiler_params=pltpu.CompilerParams(vmem_limit_bytes=40 * 1024 * 1024),
    )(cnt, sinks, q, g, kv)


def gather_kernel(
    dq_ref, dkv_ref, gs_ref,
    dqo_ref, dk_ref, dv_ref, gso_ref,
    own, mine, sums, land, gall,
    qs, qr, ms, mr, ss, sr, cs, cr, ls,
):
    me = lax.axis_index("ctx")
    y, z, c = spot(me)
    mate = me + 1 - 2 * c
    gall[me] = gs_ref[...]
    pull = pltpu.make_async_copy(dkv_ref.at[:, c], own, ls.at[0])
    pull.start()

    greet(me)

    def mate_send(i, carry):
        b = lax.rem(2 * y + z + i, 8)
        remote(dkv_ref.at[b, 1 - c], mine.at[b], ms.at[b], mr.at[b], mate).start()
        return carry

    lax.fori_loop(0, 8, mate_send, 0)

    def q_copy(to, frm):
        fy, fz, fc = spot(frm)
        rows = pl.ds(pl.multiple_of(fc * HALF, 32), HALF)
        cols = pl.ds(pl.multiple_of(fz * 512 + fy * 128, 128), 128)
        take = pl.ds(pl.multiple_of(to * HALF, 32), HALF)
        return dq_ref.at[take], dqo_ref.at[rows, cols], qs.at[to], qr.at[frm]

    a = q_copy(me, me)
    own_q = pltpu.make_async_copy(a[0], a[1], ls.at[1])
    own_q.start()

    def g_send(i, carry):
        to = lax.rem(me + i, PEERS)
        remote(gs_ref, gall.at[me], cs.at[to], cr.at[me], to).start()
        return carry

    lax.fori_loop(1, PEERS, g_send, 0)

    def q_send(i, carry):
        to = lax.rem(me + i, PEERS)
        remote(*q_copy(to, me), to).start()
        return carry

    lax.fori_loop(1, PEERS, q_send, 0)
    pull.wait()

    def chip_sum(b):
        remote(dkv_ref.at[b, c], mine.at[b], ms.at[b], mr.at[b], mate).wait_recv()
        return (own[b].astype(f32) + mine[b].astype(f32)).astype(bf16)

    def sum_send(i, carry):
        b = lax.rem(2 * y + z + i, 8)
        sums[b] = chip_sum(b)
        to = 2 * b + c
        remote(sums.at[b], land.at[2 * y + z], ss.at[b], sr.at[2 * y + z], to).start()
        return carry

    lax.fori_loop(1, 8, sum_send, 0)
    land[2 * y + z] = chip_sum(2 * y + z)

    def sum_get(i, carry):
        b = lax.rem(2 * y + z + i, 8)
        cp = remote(sums.at[b], land.at[b], ss.at[b], sr.at[b], 2 * b + c)
        cp.wait_send()
        cp.wait_recv()
        return carry

    lax.fori_loop(1, 8, sum_get, 0)
    heads = []
    for h in range(2):
        heads.append(
            (land[h].astype(f32) + land[2 + h].astype(f32))
            + (land[4 + h].astype(f32) + land[6 + h].astype(f32))
        )
    dk_ref[...] = jnp.concatenate([heads[0][:, :D], heads[1][:, :D]], axis=1).astype(bf16)
    dv_ref[...] = jnp.concatenate([heads[0][:, D:], heads[1][:, D:]], axis=1).astype(bf16)

    def rest(i, carry):
        o = lax.rem(me + i, PEERS)
        cp = remote(*q_copy(o, o), o)
        cp.wait_send()
        cp.wait_recv()
        cp = remote(gs_ref, gall.at[o], cs.at[o], cr.at[o], o)
        cp.wait_send()
        cp.wait_recv()
        return carry

    lax.fori_loop(1, PEERS, rest, 0)

    def mate_sent(b, carry):
        remote(dkv_ref.at[b, 1 - c], mine.at[b], ms.at[b], mr.at[b], mate).wait_send()
        return carry

    lax.fori_loop(0, 8, mate_sent, 0)
    own_q.wait()
    total = gall[0]
    for i in range(1, PEERS):
        total = total + gall[i]
    gso_ref[...] = total


def gather(dq, dkv, gs):
    any_ = pl.BlockSpec(memory_space=pl.ANY)
    vmem = pl.BlockSpec(memory_space=pltpu.VMEM)
    sem = pltpu.SemaphoreType.DMA
    blocks = pltpu.VMEM((8, ROWS, 128), bf16)
    return pl.pallas_call(
        gather_kernel,
        name="gather",
        out_shape=(
            jax.ShapeDtypeStruct((ROWS, 1024), bf16),
            jax.ShapeDtypeStruct((ROWS, 128), bf16),
            jax.ShapeDtypeStruct((ROWS, 128), bf16),
            jax.ShapeDtypeStruct((1, 128), f32),
        ),
        in_specs=[any_, any_, vmem],
        out_specs=(any_, vmem, vmem, vmem),
        scratch_shapes=[blocks, blocks, blocks, blocks, pltpu.VMEM((PEERS, 1, 128), f32)]
        + [sem((PEERS,))] * 2
        + [sem((8,))] * 4
        + [sem((PEERS,))] * 2
        + [sem((2,))],
        compiler_params=pltpu.CompilerParams(collective_id=1, has_side_effects=True),
    )(dq, dkv.reshape(8, 2, ROWS, 128), gs)


def on_device(queries, keys, values, grad_out, segments, sinks):
    q, g, kv, cnt = scatter(queries, grad_out, keys, values, segments.reshape(1, ROWS))
    dq, dkv, gs = local(cnt, sinks, q, g, kv)
    grad_q, dk, dv, grad_sinks = gather(dq, dkv, gs)
    return grad_q, dk, dv, grad_sinks.reshape(128)[: sinks.shape[0]]


def solution(mesh):
    rows = P(("dp", "ctx"), "tp")
    return jax.shard_map(
        on_device,
        mesh=mesh,
        in_specs=(rows, rows, rows, rows, P(("dp", "ctx")), P("tp")),
        out_specs=(rows, rows, rows, P(("dp", "tp"))),
        check_vma=False,
    )
```

```python
import functools

import jax
import jax.numpy as jnp
from jax import lax
from jax.experimental import pallas as pl
from jax.experimental.pallas import tpu as pltpu
from jax.sharding import PartitionSpec as P

D = 64
PEERS = 16
ROWS = 192
DOCS = 6
TILE = 128
LANES = 2 * TILE
UNIT = 128
SUB = 2
PAD = 4
SIZES = (2, 4, 8, 12, 16, 20)
FAR = 1 << 20
LOG2E = 1.4426950408889634
FILL = -1e30
f32 = jnp.float32
bf16 = jnp.bfloat16


def spot(i):
    return i // 4, lax.rem(i // 2, 2), lax.rem(i, 2)


def is_full(block, core):
    tile = (3 * block + lax.rem(block, 2)) // 2
    return 1 - lax.rem(tile + core, 2)


def piece(block, full):
    odd = lax.rem(block, 2)
    first = odd if full else 2 - 2 * odd
    g = 3 * block + first
    return 64 * first, (g // 4) * TILE + lax.rem(g, 2) * 64


def remote(src, dst, send, recv, to):
    return pltpu.make_async_remote_copy(
        src_ref=src,
        dst_ref=dst,
        send_sem=send,
        recv_sem=recv,
        device_id={"ctx": to},
        device_id_type=pl.DeviceIdType.MESH,
    )


def greet(me):
    barrier = pltpu.get_barrier_semaphore()

    def hello(i, c):
        to = lax.rem(me + i, PEERS)
        pl.semaphore_signal(
            barrier, inc=1, device_id={"ctx": to}, device_id_type=pl.DeviceIdType.MESH
        )
        return c

    lax.fori_loop(1, PEERS, hello, 0)
    pl.semaphore_wait(barrier, PEERS - 1)


def scatter_kernel(
    q_ref, g_ref, k_ref, v_ref, seg_ref,
    qo_ref, go_ref, kvo_ref, cnt_ref,
    kvbuf, cntbuf, cntall,
    qs, qr, gs, gr, ks, kr, fs, cs, cr, ls,
):
    me = lax.axis_index("ctx")
    y, z, c = spot(me)
    mate = me + 1 - 2 * c

    for h in range(2):
        kvbuf[h] = jnp.concatenate(
            [k_ref[:, h * D : (h + 1) * D], v_ref[:, h * D : (h + 1) * D]], axis=1
        )
    lane = lax.broadcasted_iota(jnp.int32, (1, 128), 1)
    row = jnp.zeros((1, 128), f32)
    for d in range(1, DOCS):
        below = jnp.sum(jnp.where(seg_ref[...] < d, 1.0, 0.0), axis=1, keepdims=True)
        row = jnp.where(lane == d, below, row)
    cntbuf[...] = row
    cntall[me] = row

    greet(me)

    def q_copies(to, frm, start=None):
        ty, tz, tc = spot(to)
        cols = pl.ds(pl.multiple_of(tz * 512 + ty * 128, 128), 128)

        def each(full, size):
            @pl.when(is_full(frm, tc) == full)
            def _():
                src, dst = piece(frm, full)
                rows = pl.ds(pl.multiple_of(src, 64), size)
                land = pl.ds(pl.multiple_of(dst, 64), size)
                start(q_ref.at[rows, cols], qo_ref.at[land], qs.at[to], qr.at[frm])
                start(g_ref.at[rows, cols], go_ref.at[land], gs.at[to], gr.at[frm])

        each(1, TILE)
        each(0, TILE // 2)

    def kv_at(i):
        return kvo_ref.at[pl.ds(pl.multiple_of(i * ROWS, 64), ROWS)]

    q_copies(me, me, lambda src, dst, x, sem: pltpu.make_async_copy(src, dst, sem).start())
    own_kv = pltpu.make_async_copy(kvbuf.at[z], kv_at(me), ls.at[0])
    own_kv.start()

    def kv_send(i, carry):
        to = lax.rem(me + 2 * i, PEERS)
        remote(kvbuf.at[spot(to)[1]], kv_at(me), ks.at[to], kr.at[me], to).start()
        return carry

    lax.fori_loop(1, 8, kv_send, 0)
    remote(kvbuf.at[z], kv_at(me), ks.at[mate], kr.at[me], mate).start()

    def cnt_send(i, carry):
        to = lax.rem(me + i, PEERS)
        remote(cntbuf, cntall.at[me], cs.at[to], cr.at[me], to).start()
        return carry

    lax.fori_loop(1, PEERS, cnt_send, 0)

    def q_send(i, carry):
        to = lax.rem(me + i, PEERS)
        q_copies(to, me, lambda *p: remote(*p, to).start())
        return carry

    lax.fori_loop(1, PEERS, q_send, 0)

    def kv_pass(i, carry):
        frm = lax.rem(me + PEERS - 2 * i, PEERS)
        remote(kvbuf.at[0], kv_at(frm), ks.at[frm], kr.at[frm], frm).wait_recv()
        remote(kv_at(frm), kv_at(frm), fs.at[frm], kr.at[frm], mate).start()
        return carry

    lax.fori_loop(1, 8, kv_pass, 0)

    def kv_get(i, carry):
        frm = lax.rem(mate + 2 * i, PEERS)
        remote(kvbuf.at[0], kv_at(frm), ks.at[frm], kr.at[frm], frm).wait_recv()
        return carry

    lax.fori_loop(0, 8, kv_get, 0)

    def kv_sent(i, carry):
        to = lax.rem(me + 2 * i, PEERS)
        remote(kvbuf.at[0], kv_at(me), ks.at[to], kr.at[me], to).wait_send()
        remote(kv_at(to), kv_at(to), fs.at[to], kr.at[to], mate).wait_send()
        return carry

    lax.fori_loop(1, 8, kv_sent, 0)
    remote(kvbuf.at[0], kv_at(me), ks.at[mate], kr.at[me], mate).wait_send()

    def rest(i, carry):
        o = lax.rem(me + i, PEERS)
        q_copies(o, me, lambda *p: remote(*p, o).wait_send())
        q_copies(me, o, lambda src, dst, x, sem: remote(src, dst, x, sem, o).wait_recv())
        cp = remote(cntbuf, cntall.at[o], cs.at[o], cr.at[o], o)
        cp.wait_send()
        cp.wait_recv()
        return carry

    lax.fori_loop(1, PEERS, rest, 0)
    q_copies(me, me, lambda src, dst, x, sem: pltpu.make_async_copy(src, dst, sem).wait())
    own_kv.wait()
    total = cntall[0]
    for i in range(1, PEERS):
        total = total + cntall[i]
    cnt_ref[...] = total


def scatter(q, g, k, v, seg):
    any_ = pl.BlockSpec(memory_space=pl.ANY)
    vmem = pl.BlockSpec(memory_space=pltpu.VMEM)
    sem = pltpu.SemaphoreType.DMA
    total = PEERS * ROWS
    return pl.pallas_call(
        scatter_kernel,
        name="scatter",
        out_shape=(
            jax.ShapeDtypeStruct((total // 2, 128), bf16),
            jax.ShapeDtypeStruct((total // 2, 128), bf16),
            jax.ShapeDtypeStruct((total, 128), bf16),
            jax.ShapeDtypeStruct((1, 128), f32),
        ),
        in_specs=[any_, any_, vmem, vmem, vmem],
        out_specs=(vmem, vmem, vmem, vmem),
        scratch_shapes=[
            pltpu.VMEM((2, ROWS, 128), bf16),
            pltpu.VMEM((1, 128), f32),
            pltpu.VMEM((PEERS, 1, 128), f32),
        ]
        + [sem((PEERS,))] * 9
        + [sem((1,))],
        compiler_params=pltpu.CompilerParams(collective_id=0, has_side_effects=True),
    )(q, g, k, v, seg)


def local_kernel(
    cnt_hbm, sink_hbm, q_ref, g_ref, kv_ref,
    dq_ref, dkv_ref, gs_ref,
    cnt_ref, sink_ref, kvf_ref, kt_ref, acc_ref, s_ref, dp_ref, gacc_ref, w_ref, doc_ref, sem,
):
    me = lax.axis_index("ctx")
    y, z, c = spot(me)
    total = kv_ref.shape[0]
    head = 8 * z + 2 * y
    get_cnt = pltpu.make_async_copy(cnt_hbm, cnt_ref, sem.at[0])
    get_sink = pltpu.make_async_copy(sink_hbm, sink_ref, sem.at[1])
    get_cnt.start()
    get_sink.start()
    acc_ref[...] = jnp.zeros_like(acc_ref)
    gacc_ref[...] = jnp.zeros_like(gacc_ref)
    get_cnt.wait()
    get_sink.wait()

    begins = [cnt_ref[0, d].astype(jnp.int32) for d in range(1, DOCS)]
    doc = lax.broadcasted_iota(jnp.int32, (1, 128), 1)
    starts = jnp.zeros((1, 128), jnp.int32)
    ends = jnp.full((1, 128), FAR, jnp.int32)
    for d in range(1, DOCS):
        starts = jnp.where(doc == d, begins[d - 1], starts)
        if d < DOCS - 1:
            ends = jnp.where(doc == d, begins[d], ends)
    q_starts = jnp.where((doc >= 1) & (doc < DOCS), starts, FAR)

    pad = PAD * UNIT
    kvf_ref[:pad, :128] = jnp.zeros((pad, 128), bf16)
    ahead = lax.broadcasted_iota(jnp.int32, (pad, 128), 1) == 0
    kvf_ref[:pad, 128:] = jnp.where(ahead, 1.0, 0.0).astype(bf16)
    kt_ref[:PAD] = jnp.zeros((PAD, D, UNIT), bf16)
    row_256 = lax.broadcasted_iota(jnp.int32, (256, 128), 0)

    def fill(j, carry):
        kv = kv_ref[pl.ds(pl.multiple_of(j * 256, 256), 256), :]
        at = pl.ds(pl.multiple_of(j * 256 + pad, 256), 256)
        kvf_ref[at, :128] = kv
        kvf_ref[at, 128:] = jnp.where(row_256 + j * 256 < starts, 1.0, 0.0).astype(bf16)
        kt = kv.astype(f32).T[:D].astype(bf16)
        kt_ref[2 * j + PAD] = kt[:, :UNIT]
        kt_ref[2 * j + 1 + PAD] = kt[:, UNIT:]
        return carry

    lax.fori_loop(0, total // 256, fill, 0)

    lane = lax.broadcasted_iota(jnp.int32, (1, LANES), 1)
    sink = jnp.where(lane < TILE, sink_ref[head], sink_ref[head + 1])
    row = lax.broadcasted_iota(jnp.int32, (TILE, 128), 0)
    below = lax.broadcasted_iota(jnp.int32, (UNIT, LANES), 0) <= (lane & (TILE - 1))
    nt = (((1,), (1,)), ((), ()))

    def fold(x, op):
        return op(x.reshape(x.shape[0] // 8, 8, LANES), axis=0)

    def tile(t, carry):
        n0 = pl.multiple_of(t * TILE, TILE)
        place = 2 * t + c
        p0 = place * TILE
        first = 0
        for b in begins:
            first = jnp.where(p0 >= b, b, first)
        units = place - first // UNIT + 1
        qt = (q_ref[pl.ds(n0, TILE), :].astype(f32) * 0.125).astype(bf16)
        gt = g_ref[pl.ds(n0, TILE), :]
        none = jnp.zeros((TILE, D), bf16)
        w_ref[:TILE] = jnp.concatenate([qt[:, :D], none], axis=1)
        w_ref[TILE : 2 * TILE] = jnp.concatenate([qt[:, D:], none], axis=1)
        w_ref[2 * TILE : 3 * TILE] = jnp.concatenate([none, gt[:, :D]], axis=1)
        w_ref[3 * TILE :] = jnp.concatenate([none, gt[:, D:]], axis=1)
        inside = (row + p0 >= q_starts) & (row + p0 < ends)
        doc_ref[...] = jnp.where((doc == 0) | inside, FILL, 0.0).astype(bf16)

        def run(size):
            wg = w_ref[2 * TILE :]
            docs = jnp.concatenate([doc_ref[...]] * 2, axis=0)
            wq = jnp.concatenate([w_ref[: 2 * TILE], docs], axis=1)
            u0 = place + 1 - size + PAD

            def rows(i):
                return pl.ds(pl.multiple_of((u0 + i) * UNIT, UNIT), SUB * UNIT)

            subs = list(range(0, size, SUB))[::-1]
            top = sink
            mass = jnp.zeros((8, LANES), f32)
            tops = {}
            for i in subs:
                kv = kvf_ref[rows(i), :]
                at = slice(i * UNIT, (i + SUB) * UNIT)
                s = lax.dot_general(kv, wq, nt, preferred_element_type=f32)
                dp_ref[at, :] = lax.dot_general(kv[:, :128], wg, nt, preferred_element_type=f32)
                if i + SUB == size:
                    s = jnp.concatenate(
                        [s[:-UNIT], jnp.where(below, s[-UNIT:], FILL)], axis=0
                    )
                new = jnp.maximum(top, jnp.max(fold(s, jnp.max), axis=0, keepdims=True))
                e = jnp.exp2((s - new) * LOG2E)
                s_ref[at, :] = e
                mass = mass * jnp.exp2((top - new) * LOG2E) + fold(e, jnp.sum)
                top = tops[i] = new
            sink_e = jnp.exp2((sink - top) * LOG2E)
            inv = 1.0 / (jnp.sum(mass, axis=0, keepdims=True) + sink_e)

            delta = jnp.zeros((8, LANES), f32)
            scale = {}
            for i in subs:
                at = slice(i * UNIT, (i + SUB) * UNIT)
                scale[i] = jnp.exp2((tops[i] - top) * LOG2E) * inv
                half = (s_ref[at, :] * scale[i]).astype(bf16).astype(f32)
                delta = delta + fold(half * dp_ref[at, :], jnp.sum)
            delta = jnp.sum(delta, axis=0, keepdims=True)
            gacc_ref[...] += sink_e * inv * delta

            dqt = jnp.zeros((D, LANES), f32)
            w = w_ref[...]
            for i in subs:
                at = slice(i * UNIT, (i + SUB) * UNIT)
                prob = s_ref[at, :] * scale[i]
                ds = (prob * (dp_ref[at, :] - delta)).astype(bf16)
                x = jnp.concatenate([ds, prob.astype(bf16)], axis=1)
                acc_ref[rows(i), :] += jnp.dot(x, w, preferred_element_type=f32)
                kt = jnp.concatenate([kt_ref[u0 + i + j] for j in range(SUB)], axis=1)
                dqt = dqt + jnp.dot(kt, ds, preferred_element_type=f32)
            dq = (dqt * 0.125).T
            dq = jnp.concatenate([dq[:TILE], dq[TILE:]], axis=1)
            dq_ref[pl.ds(n0, TILE), :] = dq.astype(bf16)

        for over, size in zip((0,) + SIZES[:-1], SIZES):
            pl.when((units > over) & (units <= size))(functools.partial(run, size))
        return carry

    lax.fori_loop(0, q_ref.shape[0] // TILE, tile, 0)
    dkv_ref[...] = acc_ref[pad:, :].astype(bf16)
    g = gacc_ref[...]
    ga = -jnp.sum(g[:, :TILE], axis=1, keepdims=True)
    gb = -jnp.sum(g[:, TILE:], axis=1, keepdims=True)
    gs_ref[...] = jnp.where(doc == head, ga, jnp.where(doc == head + 1, gb, 0.0))


def local(cnt, sinks, q, g, kv):
    any_ = pl.BlockSpec(memory_space=pl.ANY)
    vmem = pl.BlockSpec(memory_space=pltpu.VMEM)
    total = kv.shape[0]
    padded = total + PAD * UNIT
    return pl.pallas_call(
        local_kernel,
        name="local",
        out_shape=(
            jax.ShapeDtypeStruct(q.shape, bf16),
            jax.ShapeDtypeStruct(kv.shape, bf16),
            jax.ShapeDtypeStruct((1, 128), f32),
        ),
        in_specs=[any_, any_, vmem, vmem, vmem],
        out_specs=(vmem, vmem, vmem),
        scratch_shapes=[
            pltpu.SMEM((1, 128), f32),
            pltpu.SMEM((16,), f32),
            pltpu.VMEM((padded, 256), bf16),
            pltpu.VMEM((padded // UNIT, D, UNIT), bf16),
            pltpu.VMEM((padded, 128), f32),
            pltpu.VMEM((SIZES[-1] * UNIT, LANES), f32),
            pltpu.VMEM((SIZES[-1] * UNIT, LANES), f32),
            pltpu.VMEM((1, LANES), f32),
            pltpu.VMEM((4 * TILE, 128), bf16),
            pltpu.VMEM((TILE, 128), bf16),
            pltpu.SemaphoreType.DMA((2,)),
        ],
        compiler_params=pltpu.CompilerParams(vmem_limit_bytes=24 * 1024 * 1024),
    )(cnt, sinks, q, g, kv)


def gather_kernel(
    dq_ref, dkv_ref, gs_ref,
    dqo_ref, land, gall,
    mine, sums,
    qs, qr, ms, mr, ss, sr, cs, cr,
):
    me = lax.axis_index("ctx")
    y, z, c = spot(me)
    mate = me + 1 - 2 * c
    gall[me] = gs_ref[...]

    greet(me)

    def mate_send(i, carry):
        b = lax.rem(2 * y + z + i, 8)
        remote(dkv_ref.at[b, 1 - c], mine.at[b], ms.at[b], mr.at[b], mate).start()
        return carry

    lax.fori_loop(0, 8, mate_send, 0)

    def q_copies(to, frm, start):
        fy, fz, fc = spot(frm)
        cols = pl.ds(pl.multiple_of(fz * 512 + fy * 128, 128), 128)

        def each(full, size):
            @pl.when(is_full(to, fc) == full)
            def _():
                dst, src = piece(to, full)
                take = pl.ds(pl.multiple_of(src, 64), size)
                rows = pl.ds(pl.multiple_of(dst, 64), size)
                start(dq_ref.at[take], dqo_ref.at[rows, cols], qs.at[to], qr.at[frm])

        each(1, TILE)
        each(0, TILE // 2)

    q_copies(me, me, lambda src, dst, x, sem: pltpu.make_async_copy(src, dst, sem).start())

    def g_send(i, carry):
        to = lax.rem(me + i, PEERS)
        remote(gs_ref, gall.at[me], cs.at[to], cr.at[me], to).start()
        return carry

    lax.fori_loop(1, PEERS, g_send, 0)

    def q_send(i, carry):
        to = lax.rem(me + i, PEERS)
        q_copies(to, me, lambda *p: remote(*p, to).start())
        return carry

    lax.fori_loop(1, PEERS, q_send, 0)

    def chip_sum(b):
        remote(dkv_ref.at[b, c], mine.at[b], ms.at[b], mr.at[b], mate).wait_recv()
        return (dkv_ref[b, c].astype(f32) + mine[b].astype(f32)).astype(bf16)

    def sum_send(i, carry):
        b = lax.rem(2 * y + z + i, 8)
        sums[b] = chip_sum(b)
        to = 2 * b + c
        remote(sums.at[b], land.at[2 * y + z], ss.at[b], sr.at[2 * y + z], to).start()
        return carry

    lax.fori_loop(1, 8, sum_send, 0)
    land[2 * y + z] = chip_sum(2 * y + z)

    def sum_get(i, carry):
        b = lax.rem(2 * y + z + i, 8)
        cp = remote(sums.at[b], land.at[b], ss.at[b], sr.at[b], 2 * b + c)
        cp.wait_send()
        cp.wait_recv()
        return carry

    lax.fori_loop(1, 8, sum_get, 0)

    def rest(i, carry):
        o = lax.rem(me + i, PEERS)
        q_copies(o, me, lambda *p: remote(*p, o).wait_send())
        q_copies(me, o, lambda src, dst, x, sem: remote(src, dst, x, sem, o).wait_recv())
        cp = remote(gs_ref, gall.at[o], cs.at[o], cr.at[o], o)
        cp.wait_send()
        cp.wait_recv()
        return carry

    lax.fori_loop(1, PEERS, rest, 0)

    def mate_sent(b, carry):
        remote(dkv_ref.at[b, 1 - c], mine.at[b], ms.at[b], mr.at[b], mate).wait_send()
        return carry

    lax.fori_loop(0, 8, mate_sent, 0)
    q_copies(me, me, lambda src, dst, x, sem: pltpu.make_async_copy(src, dst, sem).wait())


def gather(dq, dkv, gs):
    vmem = pl.BlockSpec(memory_space=pltpu.VMEM)
    sem = pltpu.SemaphoreType.DMA
    blocks = pltpu.VMEM((8, ROWS, 128), bf16)
    return pl.pallas_call(
        gather_kernel,
        name="gather",
        out_shape=(
            jax.ShapeDtypeStruct((ROWS, 1024), bf16),
            jax.ShapeDtypeStruct((8, ROWS, 128), bf16),
            jax.ShapeDtypeStruct((PEERS, 1, 128), f32),
        ),
        in_specs=[vmem, vmem, vmem],
        out_specs=(vmem, vmem, vmem),
        scratch_shapes=[blocks, blocks]
        + [sem((PEERS,))] * 2
        + [sem((8,))] * 4
        + [sem((PEERS,))] * 2,
        compiler_params=pltpu.CompilerParams(collective_id=1, has_side_effects=True),
    )(dq, dkv.reshape(8, 2, ROWS, 128), gs)


def finish_kernel(dq_ref, land, gall, dqo_ref, dk_ref, dv_ref, gso_ref, sem):
    out = pltpu.make_async_copy(dq_ref, dqo_ref, sem)
    out.start()
    heads = []
    for h in range(2):
        heads.append(
            (land[h].astype(f32) + land[2 + h].astype(f32))
            + (land[4 + h].astype(f32) + land[6 + h].astype(f32))
        )
    dk_ref[...] = jnp.concatenate([heads[0][:, :D], heads[1][:, :D]], axis=1).astype(bf16)
    dv_ref[...] = jnp.concatenate([heads[0][:, D:], heads[1][:, D:]], axis=1).astype(bf16)
    total = gall[0]
    for i in range(1, PEERS):
        total = total + gall[i]
    gso_ref[...] = total
    out.wait()


def finish(dq, land, gall):
    vmem = pl.BlockSpec(memory_space=pltpu.VMEM)
    return pl.pallas_call(
        finish_kernel,
        name="finish",
        out_shape=(
            jax.ShapeDtypeStruct((ROWS, 1024), bf16),
            jax.ShapeDtypeStruct((ROWS, 128), bf16),
            jax.ShapeDtypeStruct((ROWS, 128), bf16),
            jax.ShapeDtypeStruct((1, 128), f32),
        ),
        in_specs=[vmem, vmem, vmem],
        out_specs=(pl.BlockSpec(memory_space=pl.ANY), vmem, vmem, vmem),
        scratch_shapes=[pltpu.SemaphoreType.DMA],
    )(dq, land, gall)


def on_device(queries, keys, values, grad_out, segments, sinks):
    q, g, kv, cnt = scatter(queries, grad_out, keys, values, segments.reshape(1, ROWS))
    dq, dkv, gs = local(cnt, sinks, q, g, kv)
    grad_q, dk, dv, grad_sinks = finish(*gather(dq, dkv, gs))
    return grad_q, dk, dv, grad_sinks.reshape(128)[: sinks.shape[0]]


def solution(mesh):
    rows = P(("dp", "ctx"), "tp")
    return jax.shard_map(
        on_device,
        mesh=mesh,
        in_specs=(rows, rows, rows, rows, P(("dp", "ctx")), P("tp")),
        out_specs=(rows, rows, rows, P(("dp", "tp"))),
        check_vma=False,
    )
```

```python
import functools

import jax
import jax.numpy as jnp
from jax import lax
from jax.experimental import pallas as pl
from jax.experimental.pallas import tpu as pltpu
from jax.sharding import PartitionSpec as P

D = 64
PEERS = 16
ROWS = 192
TOTAL = PEERS * ROWS
DOCS = 6
TILE = 128
TILES = TOTAL // TILE // 2
LANES = 2 * TILE
UNIT = 128
SUB = 2
PAD = 4
PADDED = TOTAL + PAD * UNIT
SIZES = (2, 4, 8, 12, 16, 20)
LOG2E = 1.4426950408889634
FILL = -1e30
f32 = jnp.float32
bf16 = jnp.bfloat16


def spot(i):
    return i // 4, lax.rem(i // 2, 2), lax.rem(i, 2)


def is_full(block, core):
    tile = (3 * block + lax.rem(block, 2)) // 2
    return 1 - lax.rem(tile + core, 2)


def piece(block, full):
    odd = lax.rem(block, 2)
    first = odd if full else 2 - 2 * odd
    g = 3 * block + first
    return 64 * first, (g // 4) * TILE + lax.rem(g, 2) * 64


def remote(src, dst, send, recv, to):
    return pltpu.make_async_remote_copy(
        src_ref=src,
        dst_ref=dst,
        send_sem=send,
        recv_sem=recv,
        device_id={"ctx": to},
        device_id_type=pl.DeviceIdType.MESH,
    )


def here(src, dst, _, sem):
    return pltpu.make_async_copy(src, dst, sem)


def greet(me):
    barrier = pltpu.get_barrier_semaphore()

    def hello(i, carry):
        to = lax.rem(me + i, PEERS)
        pl.semaphore_signal(
            barrier, inc=1, device_id={"ctx": to}, device_id_type=pl.DeviceIdType.MESH
        )
        return carry

    lax.fori_loop(1, PEERS, hello, 0)
    pl.semaphore_wait(barrier, PEERS - 1)


def fold(x, op):
    return op(x.reshape(x.shape[0] // 8, 8, LANES), axis=0)


def whole_kernel(
    q_ref, g_ref, k_ref, v_ref, seg_ref, sink_ref,
    dqo_ref, dk_ref, dv_ref, gso_ref,
    kvbuf, cntbuf, cntall, ql, gl, kvl, docl, acc_ref, s_ref, dp_ref, gacc_ref, w_ref, doc_ref,
    dqb, half, mine, sums, land, gbuf, gall,
    ks, kr, fs, cs, cr, qs, qr, gs, gr, ds, dr, es, er, ms, mr, ss, sr, ls,
):
    me = lax.axis_index("ctx")
    y, z, c = spot(me)
    chip = me // 2
    mate = me + 1 - 2 * c
    head = 8 * z + 2 * y
    pad = PAD * UNIT

    for h in range(2):
        kvbuf[h] = jnp.concatenate(
            [k_ref[:, h * D : (h + 1) * D], v_ref[:, h * D : (h + 1) * D]], axis=1
        )
    doc = lax.broadcasted_iota(jnp.int32, (1, 128), 1)
    counts = [jnp.zeros((1, 128), f32), jnp.zeros((1, 128), f32)]
    for d in range(1, DOCS):
        below = jnp.sum(jnp.where(seg_ref[...] < d, 1.0, 0.0), axis=1, keepdims=True)
        counts[0] = jnp.where(doc == d, below, counts[0])
        counts[1] = jnp.where(doc == d - 1, below, counts[1])
    for i in range(2):
        cntbuf[i] = counts[i]
        cntall[me, i] = counts[i]

    greet(me)

    def kv_at(i):
        return kvl.at[pl.ds(pl.multiple_of(i * ROWS + pad, 64), ROWS)]

    def q_copies(to, frm, go):
        ty, tz, tc = spot(to)
        cols = pl.ds(pl.multiple_of(tz * 512 + ty * 128, 128), 128)

        def each(full, size):
            @pl.when(is_full(frm, tc) == full)
            def _():
                src, dst = piece(frm, full)
                rows = pl.ds(pl.multiple_of(src, 64), size)
                at = pl.ds(pl.multiple_of(dst, 64), size)
                go(q_ref.at[rows, cols], ql.at[at], qs.at[to], qr.at[frm])
                go(g_ref.at[rows, cols], gl.at[at], gs.at[to], gr.at[frm])

        each(1, TILE)
        each(0, TILE // 2)

    def kv_send(i, carry):
        to = lax.rem(me + PEERS - 2 * i, PEERS)
        remote(kvbuf.at[spot(to)[1]], kv_at(me), ks.at[to], kr.at[me], to).start()
        return carry

    lax.fori_loop(1, 8, kv_send, 0)
    remote(kvbuf.at[z], kv_at(me), ks.at[mate], kr.at[me], mate).start()
    own_kv = pltpu.make_async_copy(kvbuf.at[z], kv_at(me), ls.at[0])
    own_kv.start()

    def cnt_send(i, carry):
        to = lax.rem(me + i, PEERS)
        remote(cntbuf, cntall.at[me], cs.at[to], cr.at[me], to).start()
        return carry

    lax.fori_loop(1, PEERS, cnt_send, 0)
    q_copies(me, me, lambda *p: here(*p).start())
    q_copies(mate, me, lambda *p: remote(*p, mate).start())

    acc_ref[...] = jnp.zeros_like(acc_ref)
    gacc_ref[...] = jnp.zeros_like(gacc_ref)
    kvl[:pad] = jnp.zeros((pad, 128), bf16)
    w_ref[...] = jnp.zeros_like(w_ref)

    def q_send(i, carry):
        for core in range(2):
            to = lax.rem(2 * chip + PEERS - 2 * i, PEERS) + core
            q_copies(to, me, lambda *p: remote(*p, to).start())
        return carry

    def kv_pass(i, carry):
        frm = lax.rem(me + 2 * i, PEERS)
        remote(kvbuf.at[0], kv_at(frm), ks.at[frm], kr.at[frm], frm).wait_recv()
        remote(kv_at(frm), kv_at(frm), fs.at[frm], kr.at[frm], mate).start()
        return carry

    lax.fori_loop(1, 8, q_send, 0)
    lax.fori_loop(1, 8, kv_pass, 0)

    def cnt_get(i, carry):
        o = lax.rem(me + i, PEERS)
        cp = remote(cntbuf, cntall.at[o], cs.at[o], cr.at[o], o)
        cp.wait_send()
        cp.wait_recv()
        return carry

    lax.fori_loop(1, PEERS, cnt_get, 0)
    starts = cntall[0, 0]
    ends = cntall[0, 1]
    for i in range(1, PEERS):
        starts = starts + cntall[i, 0]
        ends = ends + cntall[i, 1]
    starts = starts.astype(jnp.int32)
    ends = ends.astype(jnp.int32)
    far = 2 * TOTAL
    q_starts = jnp.where((doc >= 1) & (doc < DOCS), starts, far)
    q_ends = jnp.where(doc < DOCS - 1, ends, far)

    ahead = lax.broadcasted_iota(jnp.int32, (pad, 128), 1) == 0
    docl[:pad] = jnp.where(ahead, 1.0, 0.0).astype(bf16)
    row_256 = lax.broadcasted_iota(jnp.int32, (256, 128), 0)

    def fill(j, carry):
        at = pl.ds(pl.multiple_of(j * 256 + pad, 256), 256)
        docl[at] = jnp.where(row_256 + j * 256 < starts, 1.0, 0.0).astype(bf16)
        return carry

    lax.fori_loop(0, TOTAL // 256, fill, 0)

    def kv_get(i, carry):
        frm = lax.rem(mate + 2 * i, PEERS)
        remote(kvbuf.at[0], kv_at(frm), ks.at[frm], kr.at[frm], frm).wait_recv()
        return carry

    lax.fori_loop(0, 8, kv_get, 0)
    own_kv.wait()

    lane = lax.broadcasted_iota(jnp.int32, (1, LANES), 1)
    sink = jnp.where(lane < TILE, sink_ref[head], sink_ref[head + 1])
    row = lax.broadcasted_iota(jnp.int32, (TILE, 128), 0)
    causal = lax.broadcasted_iota(jnp.int32, (UNIT, LANES), 0) <= (lane & (TILE - 1))
    nt = (((1,), (1,)), ((), ()))
    tn = (((0,), (0,)), ((), ()))

    def q_wait(frm):
        @pl.when(frm == me)
        def _():
            q_copies(me, frm, lambda *p: here(*p).wait())

        @pl.when(frm != me)
        def _():
            q_copies(me, frm, lambda *p: remote(*p, frm).wait_recv())

    def dq_copies(to, frm, go):
        fy, fz, fc = spot(frm)
        cols = pl.ds(pl.multiple_of(fz * 512 + fy * 128, 128), 128)

        def each(full, size):
            @pl.when(is_full(to, fc) == full)
            def _():
                dst, src = piece(to, full)
                take = pl.ds(pl.multiple_of(src, 64), size)
                rows = pl.ds(pl.multiple_of(dst, 64), size)
                go(dqb.at[take], dqo_ref.at[rows, cols], ds.at[to], dr.at[frm])

        each(1, TILE)
        each(0, TILE // 2)

    def dq_send(to):
        @pl.when(to == me)
        def _():
            dq_copies(to, me, lambda *p: here(*p).start())

        @pl.when(to != me)
        def _():
            dq_copies(to, me, lambda *p: remote(*p, to).start())

    first_tile = (3 * chip + 1 - c) // 2

    def tile(i, carry):
        t = lax.rem(first_tile + i, TILES)
        n0 = pl.multiple_of(t * TILE, TILE)
        place = 2 * t + c
        p0 = place * TILE
        third = lax.rem(place, 3)
        src = 2 * (place // 3)
        pl.when(third <= 1)(lambda: q_wait(src))
        pl.when(third >= 1)(lambda: q_wait(src + 1))

        qt = (ql[pl.ds(n0, TILE), :].astype(f32) * 0.125).astype(bf16)
        gt = gl[pl.ds(n0, TILE), :]
        none = jnp.zeros((TILE, D), bf16)
        w_ref[:TILE] = jnp.concatenate([qt[:, :D], none], axis=1)
        w_ref[TILE : 2 * TILE] = jnp.concatenate([qt[:, D:], none], axis=1)
        w_ref[2 * TILE : 3 * TILE] = jnp.concatenate([none, gt[:, :D]], axis=1)
        w_ref[3 * TILE :] = jnp.concatenate([none, gt[:, D:]], axis=1)
        inside = (row + p0 >= q_starts) & (row + p0 < q_ends)
        doc_ref[...] = jnp.where((doc == 0) | inside, FILL, 0.0).astype(bf16)

        def run(size):
            wg = w_ref[2 * TILE :]
            docs = jnp.concatenate([doc_ref[...]] * 2, axis=0)
            wq = jnp.concatenate([w_ref[: 2 * TILE], docs], axis=1)
            u0 = place + 1 - size + PAD

            def rows(i):
                return pl.ds(pl.multiple_of((u0 + i) * UNIT, UNIT), SUB * UNIT)

            subs = list(range(0, size, SUB))[::-1]
            top = sink
            mass = jnp.zeros((8, LANES), f32)
            tops = {}
            for i in subs:
                kv = kvl[rows(i), :]
                at = slice(i * UNIT, (i + SUB) * UNIT)
                kvd = jnp.concatenate([kv, docl[rows(i), :]], axis=1)
                s = lax.dot_general(kvd, wq, nt, preferred_element_type=f32)
                dp_ref[at, :] = lax.dot_general(kv, wg, nt, preferred_element_type=f32)
                if i + SUB == size:
                    s = jnp.concatenate(
                        [s[:-UNIT], jnp.where(causal, s[-UNIT:], FILL)], axis=0
                    )
                new = jnp.maximum(top, jnp.max(fold(s, jnp.max), axis=0, keepdims=True))
                e = jnp.exp2((s - new) * LOG2E)
                s_ref[at, :] = e
                mass = mass * jnp.exp2((top - new) * LOG2E) + fold(e, jnp.sum)
                top = tops[i] = new
            sink_e = jnp.exp2((sink - top) * LOG2E)
            inv = 1.0 / (jnp.sum(mass, axis=0, keepdims=True) + sink_e)

            delta = jnp.zeros((8, LANES), f32)
            scale = {}
            for i in subs:
                at = slice(i * UNIT, (i + SUB) * UNIT)
                scale[i] = jnp.exp2((tops[i] - top) * LOG2E) * inv
                prob_half = (s_ref[at, :] * scale[i]).astype(bf16).astype(f32)
                delta = delta + fold(prob_half * dp_ref[at, :], jnp.sum)
            delta = jnp.sum(delta, axis=0, keepdims=True)
            gacc_ref[...] += sink_e * inv * delta

            dq = jnp.zeros((LANES, 128), f32)
            w = w_ref[...]
            for i in subs:
                at = slice(i * UNIT, (i + SUB) * UNIT)
                prob = s_ref[at, :] * scale[i]
                dscore = (prob * (dp_ref[at, :] - delta)).astype(bf16)
                x = jnp.concatenate([dscore, prob.astype(bf16)], axis=1)
                acc_ref[rows(i), :] += jnp.dot(x, w, preferred_element_type=f32)
                dq = dq + lax.dot_general(dscore, kvl[rows(i), :], tn, preferred_element_type=f32)
            dq = dq[:, :D] * 0.125
            dq = jnp.concatenate([dq[:TILE], dq[TILE:]], axis=1)
            dqb[pl.ds(n0, TILE), :] = dq.astype(bf16)

        need = 2 * t + 2
        for over, size in zip((0,) + SIZES[:-1], SIZES):
            fits = (need > over) & (need <= size) if size < SIZES[-1] else need > over
            pl.when(fits)(functools.partial(run, size))
        pl.when(third <= 1)(lambda: dq_send(src))
        pl.when(third >= 1)(lambda: dq_send(src + 1))
        return carry

    lax.fori_loop(0, TILES, tile, 0)

    def block(b, core):
        return pl.ds(pl.multiple_of((2 * b + core) * ROWS + pad, 64), ROWS)

    def mate_send(i, carry):
        b = lax.rem(2 * y + z + 8 - i, 8)
        half[b] = acc_ref[block(b, 1 - c), :].astype(bf16)
        remote(half.at[b], mine.at[b], ms.at[b], mr.at[b], mate).start()
        return carry

    lax.fori_loop(1, 9, mate_send, 0)

    g = gacc_ref[...]
    ga = -jnp.sum(g[:, :TILE], axis=1, keepdims=True)
    gb = -jnp.sum(g[:, TILE:], axis=1, keepdims=True)
    g_row = jnp.where(doc == head, ga, jnp.where(doc == head + 1, gb, 0.0))
    gbuf[...] = g_row
    gall[me] = g_row

    def g_send(i, carry):
        to = lax.rem(me + i, PEERS)
        remote(gbuf, gall.at[me], es.at[to], er.at[me], to).start()
        return carry

    lax.fori_loop(1, PEERS, g_send, 0)

    def chip_sum(b):
        remote(half.at[b], mine.at[b], ms.at[b], mr.at[b], mate).wait_recv()
        return (acc_ref[block(b, c), :] + mine[b].astype(f32)).astype(bf16)

    def sum_send(i, carry):
        b = lax.rem(2 * y + z + 8 - i, 8)
        sums[b] = chip_sum(b)
        to = 2 * b + c
        remote(sums.at[b], land.at[2 * y + z], ss.at[b], sr.at[2 * y + z], to).start()
        return carry

    lax.fori_loop(1, 8, sum_send, 0)
    land[2 * y + z] = chip_sum(2 * y + z)

    def kv_sent(i, carry):
        to = lax.rem(me + 2 * i, PEERS)
        remote(kvbuf.at[0], kv_at(me), ks.at[to], kr.at[me], to).wait_send()
        remote(kv_at(to), kv_at(to), fs.at[to], kr.at[to], mate).wait_send()
        return carry

    lax.fori_loop(1, 8, kv_sent, 0)
    remote(kvbuf.at[0], kv_at(me), ks.at[mate], kr.at[me], mate).wait_send()

    def mate_sent(b, carry):
        remote(half.at[b], mine.at[b], ms.at[b], mr.at[b], mate).wait_send()
        return carry

    lax.fori_loop(0, 8, mate_sent, 0)

    def rest(i, carry):
        o = lax.rem(me + i, PEERS)
        q_copies(o, me, lambda *p: remote(*p, o).wait_send())
        dq_copies(o, me, lambda *p: remote(*p, o).wait_send())
        dq_copies(me, o, lambda *p: remote(*p, o).wait_recv())
        cp = remote(gbuf, gall.at[o], es.at[o], er.at[o], o)
        cp.wait_send()
        cp.wait_recv()
        return carry

    lax.fori_loop(1, PEERS, rest, 0)
    dq_copies(me, me, lambda *p: here(*p).wait())
    total = gall[0]
    for i in range(1, PEERS):
        total = total + gall[i]
    gso_ref[...] = total

    def sum_get(i, carry):
        b = lax.rem(2 * y + z + i, 8)
        cp = remote(sums.at[b], land.at[b], ss.at[b], sr.at[b], 2 * b + c)
        cp.wait_send()
        cp.wait_recv()
        return carry

    lax.fori_loop(1, 8, sum_get, 0)
    heads = []
    for h in range(2):
        heads.append(
            (land[h].astype(f32) + land[2 + h].astype(f32))
            + (land[4 + h].astype(f32) + land[6 + h].astype(f32))
        )
    dk_ref[...] = jnp.concatenate([heads[0][:, :D], heads[1][:, :D]], axis=1).astype(bf16)
    dv_ref[...] = jnp.concatenate([heads[0][:, D:], heads[1][:, D:]], axis=1).astype(bf16)


def whole(q, g, k, v, seg, sinks):
    any_ = pl.BlockSpec(memory_space=pl.ANY)
    vmem = pl.BlockSpec(memory_space=pltpu.VMEM)
    smem = pl.BlockSpec(memory_space=pltpu.SMEM)
    sem = pltpu.SemaphoreType.DMA
    blocks = pltpu.VMEM((8, ROWS, 128), bf16)
    longest = SIZES[-1] * UNIT
    return pl.pallas_call(
        whole_kernel,
        name="whole",
        out_shape=(
            jax.ShapeDtypeStruct((ROWS, 1024), bf16),
            jax.ShapeDtypeStruct((ROWS, 128), bf16),
            jax.ShapeDtypeStruct((ROWS, 128), bf16),
            jax.ShapeDtypeStruct((1, 128), f32),
        ),
        in_specs=[any_, any_, vmem, vmem, vmem, smem],
        out_specs=(any_, vmem, vmem, vmem),
        scratch_shapes=[
            pltpu.VMEM((2, ROWS, 128), bf16),
            pltpu.VMEM((2, 1, 128), f32),
            pltpu.VMEM((PEERS, 2, 1, 128), f32),
            pltpu.VMEM((TOTAL // 2, 128), bf16),
            pltpu.VMEM((TOTAL // 2, 128), bf16),
            pltpu.VMEM((PADDED, 128), bf16),
            pltpu.VMEM((PADDED, 128), bf16),
            pltpu.VMEM((PADDED, 128), f32),
            pltpu.VMEM((longest, LANES), f32),
            pltpu.VMEM((longest, LANES), f32),
            pltpu.VMEM((1, LANES), f32),
            pltpu.VMEM((4 * TILE, 128), bf16),
            pltpu.VMEM((TILE, 128), bf16),
            pltpu.VMEM((TOTAL // 2, 128), bf16),
            blocks,
            blocks,
            blocks,
            blocks,
            pltpu.VMEM((1, 128), f32),
            pltpu.VMEM((PEERS, 1, 128), f32),
        ]
        + [sem((PEERS,))] * 13
        + [sem((8,))] * 4
        + [sem((1,))],
        compiler_params=pltpu.CompilerParams(
            collective_id=0, has_side_effects=True, vmem_limit_bytes=32 * 1024 * 1024
        ),
    )(q, g, k, v, seg, sinks)


def on_device(queries, keys, values, grad_out, segments, sinks):
    grad_q, dk, dv, grad_sinks = whole(
        queries, grad_out, keys, values, segments.reshape(1, ROWS), sinks
    )
    return grad_q, dk, dv, grad_sinks.reshape(128)[: sinks.shape[0]]


def solution(mesh):
    rows = P(("dp", "ctx"), "tp")
    return jax.shard_map(
        on_device,
        mesh=mesh,
        in_specs=(rows, rows, rows, rows, P(("dp", "ctx")), P("tp")),
        out_specs=(rows, rows, rows, P(("dp", "tp"))),
        check_vma=False,
    )
```

```python
import functools

import jax
import jax.numpy as jnp
from jax import lax
from jax.experimental import pallas as pl
from jax.experimental.pallas import tpu as pltpu
from jax.sharding import PartitionSpec as P

D = 64
PEERS = 16
ROWS = 192
TOTAL = PEERS * ROWS
DOCS = 6
TILE = 128
TILES = TOTAL // TILE // 2
LANES = 2 * TILE
UNIT = 128
SUB = 2
PAD = 4
PADDED = TOTAL + PAD * UNIT
SIZES = (2, 4, 8, 12, 16, 20)
GRANT = 63 * 1024 * 1024
LOG2E = 1.4426950408889634
FILL = -1e30
f32 = jnp.float32
bf16 = jnp.bfloat16


def spot(i):
    return i // 4, lax.rem(i // 2, 2), lax.rem(i, 2)


def is_full(block, core):
    tile = (3 * block + lax.rem(block, 2)) // 2
    return 1 - lax.rem(tile + core, 2)


def piece(block, full):
    odd = lax.rem(block, 2)
    first = odd if full else 2 - 2 * odd
    g = 3 * block + first
    return 64 * first, (g // 4) * TILE + lax.rem(g, 2) * 64


def remote(src, dst, send, recv, to):
    return pltpu.make_async_remote_copy(
        src_ref=src,
        dst_ref=dst,
        send_sem=send,
        recv_sem=recv,
        device_id={"ctx": to},
        device_id_type=pl.DeviceIdType.MESH,
    )


def here(src, dst, _, sem):
    return pltpu.make_async_copy(src, dst, sem)


def greet(me):
    def hello(i, carry):
        to = lax.rem(me + i, PEERS)
        pl.semaphore_signal(
            pltpu.get_barrier_semaphore(),
            inc=1,
            device_id={"ctx": to},
            device_id_type=pl.DeviceIdType.MESH,
        )
        return carry

    lax.fori_loop(1, PEERS, hello, 0)


def fold(x, op):
    return op(x.reshape(x.shape[0] // 8, 8, LANES), axis=0)


def whole_kernel(
    q_ref, g_ref, k_hbm, v_hbm, seg_hbm, sink_hbm,
    dqo_ref, dk_ref, dv_ref, gso_ref,
    k_ref, v_ref, seg_ref, sink_ref, kvbuf, cntbuf, cntall, ql, gl, kvl, docl, acc_ref, s_ref, dp_ref, gacc_ref, w_ref, doc_ref,
    dqb, half, mine, sums, land, gbuf, gall,
    ks, kr, fs, cs, cr, qs, qr, gs, gr, ds, dr, es, er, ms, mr, ss, sr, ls,
):
    me = lax.axis_index("ctx")
    y, z, c = spot(me)
    chip = me // 2
    mate = me + 1 - 2 * c
    head = 8 * z + 2 * y
    pad = PAD * UNIT

    greet(me)
    fetch = [
        pltpu.make_async_copy(src, dst, ls.at[1 + i])
        for i, (src, dst) in enumerate(
            [(k_hbm, k_ref), (v_hbm, v_ref), (seg_hbm, seg_ref), (sink_hbm, sink_ref)]
        )
    ]
    for f in fetch:
        f.start()
    acc_ref[...] = jnp.zeros_like(acc_ref)
    gacc_ref[...] = jnp.zeros_like(gacc_ref)
    kvl[:pad] = jnp.zeros((pad, 128), bf16)
    for f in fetch:
        f.wait()

    for h in range(2):
        kvbuf[h] = jnp.concatenate(
            [k_ref[:, h * D : (h + 1) * D], v_ref[:, h * D : (h + 1) * D]], axis=1
        )
    doc = lax.broadcasted_iota(jnp.int32, (1, 128), 1)
    counts = [jnp.zeros((1, 128), f32), jnp.zeros((1, 128), f32)]
    for d in range(1, DOCS):
        below = jnp.sum(jnp.where(seg_ref[...] < d, 1.0, 0.0), axis=1, keepdims=True)
        counts[0] = jnp.where(doc == d, below, counts[0])
        counts[1] = jnp.where(doc == d - 1, below, counts[1])
    for i in range(2):
        cntbuf[i] = counts[i]
        cntall[me, i] = counts[i]

    pl.semaphore_wait(pltpu.get_barrier_semaphore(), PEERS - 1)

    def kv_at(i):
        return kvl.at[pl.ds(pl.multiple_of(i * ROWS + pad, 64), ROWS)]

    def q_copies(to, frm, go):
        ty, tz, tc = spot(to)
        cols = pl.ds(pl.multiple_of(tz * 512 + ty * 128, 128), 128)

        def each(full, size):
            @pl.when(is_full(frm, tc) == full)
            def _():
                src, dst = piece(frm, full)
                rows = pl.ds(pl.multiple_of(src, 64), size)
                at = pl.ds(pl.multiple_of(dst, 64), size)
                go(q_ref.at[rows, cols], ql.at[at], qs.at[to], qr.at[frm])
                go(g_ref.at[rows, cols], gl.at[at], gs.at[to], gr.at[frm])

        each(1, TILE)
        each(0, TILE // 2)

    def kv_send(i, carry):
        to = lax.rem(me + PEERS - 2 * i, PEERS)
        remote(kvbuf.at[spot(to)[1]], kv_at(me), ks.at[to], kr.at[me], to).start()
        return carry

    lax.fori_loop(1, 8, kv_send, 0)
    remote(kvbuf.at[z], kv_at(me), ks.at[mate], kr.at[me], mate).start()
    own_kv = pltpu.make_async_copy(kvbuf.at[z], kv_at(me), ls.at[0])
    own_kv.start()

    def cnt_send(i, carry):
        to = lax.rem(me + i, PEERS)
        remote(cntbuf, cntall.at[me], cs.at[to], cr.at[me], to).start()
        return carry

    lax.fori_loop(1, PEERS, cnt_send, 0)
    q_copies(me, me, lambda *p: here(*p).start())
    q_copies(mate, me, lambda *p: remote(*p, mate).start())

    def q_send(i, carry):
        for core in range(2):
            to = lax.rem(2 * chip + PEERS - 2 * i, PEERS) + core
            q_copies(to, me, lambda *p: remote(*p, to).start())
        return carry

    def kv_pass(i, carry):
        frm = lax.rem(me + 2 * i, PEERS)
        remote(kvbuf.at[0], kv_at(frm), ks.at[frm], kr.at[frm], frm).wait_recv()
        remote(kv_at(frm), kv_at(frm), fs.at[frm], kr.at[frm], mate).start()
        return carry

    lax.fori_loop(1, 8, q_send, 0)
    lax.fori_loop(1, 8, kv_pass, 0)

    def cnt_get(i, carry):
        o = lax.rem(me + i, PEERS)
        cp = remote(cntbuf, cntall.at[o], cs.at[o], cr.at[o], o)
        cp.wait_send()
        cp.wait_recv()
        return carry

    lax.fori_loop(1, PEERS, cnt_get, 0)
    starts = cntall[0, 0]
    ends = cntall[0, 1]
    for i in range(1, PEERS):
        starts = starts + cntall[i, 0]
        ends = ends + cntall[i, 1]
    starts = starts.astype(jnp.int32)
    ends = ends.astype(jnp.int32)
    far = 2 * TOTAL
    q_starts = jnp.where((doc >= 1) & (doc < DOCS), starts, far)
    q_ends = jnp.where(doc < DOCS - 1, ends, far)

    ahead = lax.broadcasted_iota(jnp.int32, (pad, 128), 1) == 0
    docl[:pad] = jnp.where(ahead, 1.0, 0.0).astype(bf16)
    row_256 = lax.broadcasted_iota(jnp.int32, (256, 128), 0)

    def fill(j, carry):
        at = pl.ds(pl.multiple_of(j * 256 + pad, 256), 256)
        docl[at] = jnp.where(row_256 + j * 256 < starts, 1.0, 0.0).astype(bf16)
        return carry

    lax.fori_loop(0, TOTAL // 256, fill, 0)

    def kv_get(i, carry):
        frm = lax.rem(mate + 2 * i, PEERS)
        remote(kvbuf.at[0], kv_at(frm), ks.at[frm], kr.at[frm], frm).wait_recv()
        return carry

    lax.fori_loop(0, 8, kv_get, 0)
    own_kv.wait()

    lane = lax.broadcasted_iota(jnp.int32, (1, LANES), 1)
    sink = jnp.where(lane < TILE, sink_ref[head], sink_ref[head + 1])
    row = lax.broadcasted_iota(jnp.int32, (TILE, 128), 0)
    causal = lax.broadcasted_iota(jnp.int32, (UNIT, LANES), 0) <= (lane & (TILE - 1))
    nt = (((1,), (1,)), ((), ()))
    tn = (((0,), (0,)), ((), ()))

    def q_wait(frm):
        @pl.when(frm == me)
        def _():
            q_copies(me, frm, lambda *p: here(*p).wait())

        @pl.when(frm != me)
        def _():
            q_copies(me, frm, lambda *p: remote(*p, frm).wait_recv())

    def dq_copies(to, frm, go):
        fy, fz, fc = spot(frm)
        cols = pl.ds(pl.multiple_of(fz * 512 + fy * 128, 128), 128)

        def each(full, size):
            @pl.when(is_full(to, fc) == full)
            def _():
                dst, src = piece(to, full)
                take = pl.ds(pl.multiple_of(src, 64), size)
                rows = pl.ds(pl.multiple_of(dst, 64), size)
                go(dqb.at[take], dqo_ref.at[rows, cols], ds.at[to], dr.at[frm])

        each(1, TILE)
        each(0, TILE // 2)

    def dq_send(to):
        @pl.when(to == me)
        def _():
            dq_copies(to, me, lambda *p: here(*p).start())

        @pl.when(to != me)
        def _():
            dq_copies(to, me, lambda *p: remote(*p, to).start())

    first_tile = (3 * chip + 1 - c) // 2

    def tile(i, carry):
        t = lax.rem(first_tile + i, TILES)
        n0 = pl.multiple_of(t * TILE, TILE)
        place = 2 * t + c
        p0 = place * TILE
        third = lax.rem(place, 3)
        src = 2 * (place // 3)
        pl.when(third <= 1)(lambda: q_wait(src))
        pl.when(third >= 1)(lambda: q_wait(src + 1))

        qt = (ql[pl.ds(n0, TILE), :].astype(f32) * 0.125).astype(bf16)
        gt = gl[pl.ds(n0, TILE), :]
        none = jnp.zeros((TILE, D), bf16)
        w_ref[:TILE] = jnp.concatenate([qt[:, :D], none], axis=1)
        w_ref[TILE : 2 * TILE] = jnp.concatenate([qt[:, D:], none], axis=1)
        w_ref[2 * TILE : 3 * TILE] = jnp.concatenate([none, gt[:, :D]], axis=1)
        w_ref[3 * TILE :] = jnp.concatenate([none, gt[:, D:]], axis=1)
        inside = (row + p0 >= q_starts) & (row + p0 < q_ends)
        doc_ref[...] = jnp.where((doc == 0) | inside, FILL, 0.0).astype(bf16)

        def run(size):
            wg = w_ref[2 * TILE :]
            docs = jnp.concatenate([doc_ref[...]] * 2, axis=0)
            wq = jnp.concatenate([w_ref[: 2 * TILE], docs], axis=1)
            u0 = place + 1 - size + PAD

            def rows(i):
                return pl.ds(pl.multiple_of((u0 + i) * UNIT, UNIT), SUB * UNIT)

            subs = list(range(0, size, SUB))[::-1]
            top = sink
            mass = jnp.zeros((8, LANES), f32)
            tops = {}
            for i in subs:
                kv = kvl[rows(i), :]
                at = slice(i * UNIT, (i + SUB) * UNIT)
                kvd = jnp.concatenate([kv, docl[rows(i), :]], axis=1)
                s = lax.dot_general(kvd, wq, nt, preferred_element_type=f32)
                dp_ref[at, :] = lax.dot_general(kv, wg, nt, preferred_element_type=f32)
                if i + SUB == size:
                    s = jnp.concatenate(
                        [s[:-UNIT], jnp.where(causal, s[-UNIT:], FILL)], axis=0
                    )
                new = jnp.maximum(top, jnp.max(fold(s, jnp.max), axis=0, keepdims=True))
                e = jnp.exp2((s - new) * LOG2E)
                s_ref[at, :] = e
                mass = mass * jnp.exp2((top - new) * LOG2E) + fold(e, jnp.sum)
                top = tops[i] = new
            sink_e = jnp.exp2((sink - top) * LOG2E)
            inv = 1.0 / (jnp.sum(mass, axis=0, keepdims=True) + sink_e)

            delta = jnp.zeros((8, LANES), f32)
            scale = {}
            for i in subs:
                at = slice(i * UNIT, (i + SUB) * UNIT)
                scale[i] = jnp.exp2((tops[i] - top) * LOG2E) * inv
                prob_half = (s_ref[at, :] * scale[i]).astype(bf16).astype(f32)
                delta = delta + fold(prob_half * dp_ref[at, :], jnp.sum)
            delta = jnp.sum(delta, axis=0, keepdims=True)
            gacc_ref[...] += sink_e * inv * delta

            dq = jnp.zeros((LANES, 128), f32)
            w = w_ref[...]
            for i in subs:
                at = slice(i * UNIT, (i + SUB) * UNIT)
                prob = s_ref[at, :] * scale[i]
                dscore = (prob * (dp_ref[at, :] - delta)).astype(bf16)
                x = jnp.concatenate([dscore, prob.astype(bf16)], axis=1)
                acc_ref[rows(i), :] += jnp.dot(x, w, preferred_element_type=f32)
                dq = dq + lax.dot_general(dscore, kvl[rows(i), :], tn, preferred_element_type=f32)
            dq = dq[:, :D] * 0.125
            dq = jnp.concatenate([dq[:TILE], dq[TILE:]], axis=1)
            dqb[pl.ds(n0, TILE), :] = dq.astype(bf16)

        need = 2 * t + 2
        for over, size in zip((0,) + SIZES[:-1], SIZES):
            fits = (need > over) & (need <= size) if size < SIZES[-1] else need > over
            pl.when(fits)(functools.partial(run, size))
        pl.when(third <= 1)(lambda: dq_send(src))
        pl.when(third >= 1)(lambda: dq_send(src + 1))
        return carry

    lax.fori_loop(0, TILES, tile, 0)

    def block(b, core):
        return pl.ds(pl.multiple_of((2 * b + core) * ROWS + pad, 64), ROWS)

    def mate_send(i, carry):
        b = lax.rem(2 * y + z + 8 - i, 8)
        half[b] = acc_ref[block(b, 1 - c), :].astype(bf16)
        remote(half.at[b], mine.at[b], ms.at[b], mr.at[b], mate).start()
        return carry

    lax.fori_loop(1, 9, mate_send, 0)

    g = gacc_ref[...]
    ga = -jnp.sum(g[:, :TILE], axis=1, keepdims=True)
    gb = -jnp.sum(g[:, TILE:], axis=1, keepdims=True)
    g_row = jnp.where(doc == head, ga, jnp.where(doc == head + 1, gb, 0.0))
    gbuf[...] = g_row
    gall[me] = g_row

    def g_send(i, carry):
        to = lax.rem(me + i, PEERS)
        remote(gbuf, gall.at[me], es.at[to], er.at[me], to).start()
        return carry

    lax.fori_loop(1, PEERS, g_send, 0)

    def chip_sum(b):
        remote(half.at[b], mine.at[b], ms.at[b], mr.at[b], mate).wait_recv()
        return (acc_ref[block(b, c), :] + mine[b].astype(f32)).astype(bf16)

    def sum_send(i, carry):
        b = lax.rem(2 * y + z + 8 - i, 8)
        sums[b] = chip_sum(b)
        to = 2 * b + c
        remote(sums.at[b], land.at[2 * y + z], ss.at[b], sr.at[2 * y + z], to).start()
        return carry

    lax.fori_loop(1, 8, sum_send, 0)
    land[2 * y + z] = chip_sum(2 * y + z)

    def kv_sent(i, carry):
        to = lax.rem(me + 2 * i, PEERS)
        remote(kvbuf.at[0], kv_at(me), ks.at[to], kr.at[me], to).wait_send()
        remote(kv_at(to), kv_at(to), fs.at[to], kr.at[to], mate).wait_send()
        return carry

    lax.fori_loop(1, 8, kv_sent, 0)
    remote(kvbuf.at[0], kv_at(me), ks.at[mate], kr.at[me], mate).wait_send()

    def mate_sent(b, carry):
        remote(half.at[b], mine.at[b], ms.at[b], mr.at[b], mate).wait_send()
        return carry

    lax.fori_loop(0, 8, mate_sent, 0)

    def rest(i, carry):
        o = lax.rem(me + i, PEERS)
        q_copies(o, me, lambda *p: remote(*p, o).wait_send())
        dq_copies(o, me, lambda *p: remote(*p, o).wait_send())
        dq_copies(me, o, lambda *p: remote(*p, o).wait_recv())
        cp = remote(gbuf, gall.at[o], es.at[o], er.at[o], o)
        cp.wait_send()
        cp.wait_recv()
        return carry

    lax.fori_loop(1, PEERS, rest, 0)
    dq_copies(me, me, lambda *p: here(*p).wait())
    total = gall[0]
    for i in range(1, PEERS):
        total = total + gall[i]
    gso_ref[...] = total[0, :16]

    def sum_get(i, carry):
        b = lax.rem(2 * y + z + i, 8)
        cp = remote(sums.at[b], land.at[b], ss.at[b], sr.at[b], 2 * b + c)
        cp.wait_send()
        cp.wait_recv()
        return carry

    lax.fori_loop(1, 8, sum_get, 0)
    heads = []
    for h in range(2):
        heads.append(
            (land[h].astype(f32) + land[2 + h].astype(f32))
            + (land[4 + h].astype(f32) + land[6 + h].astype(f32))
        )
    dk_ref[...] = jnp.concatenate([heads[0][:, :D], heads[1][:, :D]], axis=1).astype(bf16)
    dv_ref[...] = jnp.concatenate([heads[0][:, D:], heads[1][:, D:]], axis=1).astype(bf16)


def whole(q, g, k, v, seg, sinks):
    hbm = pl.BlockSpec(memory_space=pltpu.HBM)
    vmem = pl.BlockSpec(memory_space=pltpu.VMEM)
    sem = pltpu.SemaphoreType.DMA
    blocks = pltpu.VMEM((8, ROWS, 128), bf16)
    longest = SIZES[-1] * UNIT
    return pl.pallas_call(
        whole_kernel,
        name="whole",
        out_shape=(
            jax.ShapeDtypeStruct((ROWS, 1024), bf16),
            jax.ShapeDtypeStruct((ROWS, 128), bf16),
            jax.ShapeDtypeStruct((ROWS, 128), bf16),
            jax.ShapeDtypeStruct((16,), f32),
        ),
        in_specs=[hbm] * 6,
        out_specs=(hbm, vmem, vmem, vmem),
        scratch_shapes=[
            pltpu.VMEM((ROWS, 128), bf16),
            pltpu.VMEM((ROWS, 128), bf16),
            pltpu.VMEM((1, ROWS), jnp.int32),
            pltpu.SMEM((16,), f32),
            pltpu.VMEM((2, ROWS, 128), bf16),
            pltpu.VMEM((2, 1, 128), f32),
            pltpu.VMEM((PEERS, 2, 1, 128), f32),
            pltpu.VMEM((TOTAL // 2, 128), bf16),
            pltpu.VMEM((TOTAL // 2, 128), bf16),
            pltpu.VMEM((PADDED, 128), bf16),
            pltpu.VMEM((PADDED, 128), bf16),
            pltpu.VMEM((PADDED, 128), f32),
            pltpu.VMEM((longest, LANES), f32),
            pltpu.VMEM((longest, LANES), f32),
            pltpu.VMEM((1, LANES), f32),
            pltpu.VMEM((4 * TILE, 128), bf16),
            pltpu.VMEM((TILE, 128), bf16),
            pltpu.VMEM((TOTAL // 2, 128), bf16),
            blocks,
            blocks,
            blocks,
            blocks,
            pltpu.VMEM((1, 128), f32),
            pltpu.VMEM((PEERS, 1, 128), f32),
        ]
        + [sem((PEERS,))] * 13
        + [sem((8,))] * 4
        + [sem((5,))],
        compiler_params=pltpu.CompilerParams(
            collective_id=0, has_side_effects=True, vmem_limit_bytes=GRANT
        ),
    )(q, g, k, v, seg, sinks)


def hand_over_kernel(*refs):
    sems = refs[-2:]
    n = (len(refs) - 2) // 3
    moves = []
    for i in range(n):
        src, dst, via = refs[i], refs[n + i], refs[2 * n + i]
        parts = [pl.ds(r, 48) for r in range(0, ROWS, 48)] if src.shape[1:] == (1024,) else [None]
        for part in parts:
            ref = [r if part is None else r.at[part] for r in (src, via, dst)]
            k = len(moves)
            moves.append(
                (
                    pltpu.make_async_copy(ref[0], ref[1], sems[0].at[k]),
                    pltpu.make_async_copy(ref[1], ref[2], sems[1].at[k]),
                )
            )
    for come, _ in moves:
        come.start()
    for come, go in moves:
        come.wait()
        go.start()
    for _, go in moves:
        go.wait()


def hand_over(*arrays):
    hbm = pl.BlockSpec(memory_space=pltpu.HBM)
    shapes = [(a.shape, a.dtype) for a in arrays]
    return pl.pallas_call(
        hand_over_kernel,
        name="hand_over",
        out_shape=tuple(jax.ShapeDtypeStruct(*a) for a in shapes),
        in_specs=[hbm] * len(arrays),
        out_specs=(hbm,) * len(arrays),
        scratch_shapes=[pltpu.VMEM(*a) for a in shapes]
        + [pltpu.SemaphoreType.DMA((16,))] * 2,
        compiler_params=pltpu.CompilerParams(vmem_limit_bytes=GRANT),
    )(*arrays)


def on_device(queries, keys, values, grad_out, segments, sinks):
    grad_q, dk, dv, grad_sinks = whole(
        queries, grad_out, keys, values, segments.reshape(1, ROWS), sinks
    )
    return hand_over(grad_q, dk, dv, grad_sinks)


def solution(mesh):
    rows = P(("dp", "ctx"), "tp")
    return jax.shard_map(
        on_device,
        mesh=mesh,
        in_specs=(rows, rows, rows, rows, P(("dp", "ctx")), P("tp")),
        out_specs=(rows, rows, rows, P(("dp", "tp"))),
        check_vma=False,
    )
```

```python
import functools

import jax
import jax.numpy as jnp
from jax import lax
from jax.experimental import pallas as pl
from jax.experimental.pallas import tpu as pltpu
from jax.sharding import PartitionSpec as P

D = 64
PEERS = 16
ROWS = 192
TOTAL = PEERS * ROWS
DOCS = 6
TILE = 128
TILES = TOTAL // TILE // 2
LANES = 2 * TILE
UNIT = 128
SUB = 2
PAD = 4
PADDED = TOTAL + PAD * UNIT
LONGEST = 20
GRANT = 63 * 1024 * 1024
LOG2E = 1.4426950408889634
FILL = -1e30
f32 = jnp.float32
bf16 = jnp.bfloat16


def spot(i):
    return i // 4, lax.rem(i // 2, 2), lax.rem(i, 2)


def is_full(block, core):
    tile = (3 * block + lax.rem(block, 2)) // 2
    return 1 - lax.rem(tile + core, 2)


def piece(block, full):
    odd = lax.rem(block, 2)
    first = odd if full else 2 - 2 * odd
    g = 3 * block + first
    return 64 * first, (g // 4) * TILE + lax.rem(g, 2) * 64


def remote(src, dst, send, recv, to):
    return pltpu.make_async_remote_copy(
        src_ref=src,
        dst_ref=dst,
        send_sem=send,
        recv_sem=recv,
        device_id={"ctx": to},
        device_id_type=pl.DeviceIdType.MESH,
    )


def here(src, dst, _, sem):
    return pltpu.make_async_copy(src, dst, sem)


def greet(me):
    def hello(i, carry):
        to = lax.rem(me + i, PEERS)
        pl.semaphore_signal(
            pltpu.get_barrier_semaphore(),
            inc=1,
            device_id={"ctx": to},
            device_id_type=pl.DeviceIdType.MESH,
        )
        return carry

    lax.fori_loop(1, PEERS, hello, 0)


def fold(x, op):
    return op(x.reshape(x.shape[0] // 8, 8, LANES), axis=0)


def whole_kernel(
    q_ref, g_ref, k_hbm, v_hbm, seg_hbm, sink_hbm,
    dqo_ref, dk_ref, dv_ref, gso_ref,
    k_ref, v_ref, seg_ref, sink_ref, kvbuf, cntbuf, cntall, ql, gl, kvl, docl, acc_ref, s_ref, dp_ref, gacc_ref, w_ref, doc_ref,
    dqb, half, mine, sums, land, gbuf, gall,
    ks, kr, fs, cs, cr, qs, qr, gs, gr, ds, dr, es, er, ms, mr, ss, sr, ls,
):
    me = lax.axis_index("ctx")
    y, z, c = spot(me)
    chip = me // 2
    mate = me + 1 - 2 * c
    head = 8 * z + 2 * y
    pad = PAD * UNIT

    greet(me)
    fetch = [
        pltpu.make_async_copy(src, dst, ls.at[1 + i])
        for i, (src, dst) in enumerate(
            [(k_hbm, k_ref), (v_hbm, v_ref), (seg_hbm, seg_ref), (sink_hbm, sink_ref)]
        )
    ]
    for f in fetch:
        f.start()
    acc_ref[...] = jnp.zeros_like(acc_ref)
    gacc_ref[...] = jnp.zeros_like(gacc_ref)
    kvl[:pad] = jnp.zeros((pad, 128), bf16)
    for f in fetch:
        f.wait()

    for h in range(2):
        kvbuf[h] = jnp.concatenate(
            [k_ref[:, h * D : (h + 1) * D], v_ref[:, h * D : (h + 1) * D]], axis=1
        )
    doc = lax.broadcasted_iota(jnp.int32, (1, 128), 1)
    counts = [jnp.zeros((1, 128), f32), jnp.zeros((1, 128), f32)]
    for d in range(1, DOCS):
        below = jnp.sum(jnp.where(seg_ref[...] < d, 1.0, 0.0), axis=1, keepdims=True)
        counts[0] = jnp.where(doc == d, below, counts[0])
        counts[1] = jnp.where(doc == d - 1, below, counts[1])
    for i in range(2):
        cntbuf[i] = counts[i]
        cntall[me, i] = counts[i]

    pl.semaphore_wait(pltpu.get_barrier_semaphore(), PEERS - 1)

    def kv_at(i):
        return kvl.at[pl.ds(pl.multiple_of(i * ROWS + pad, 64), ROWS)]

    def q_copies(to, frm, go):
        ty, tz, tc = spot(to)
        cols = pl.ds(pl.multiple_of(tz * 512 + ty * 128, 128), 128)

        def each(full, size):
            @pl.when(is_full(frm, tc) == full)
            def _():
                src, dst = piece(frm, full)
                rows = pl.ds(pl.multiple_of(src, 64), size)
                at = pl.ds(pl.multiple_of(dst, 64), size)
                go(q_ref.at[rows, cols], ql.at[at], qs.at[to], qr.at[frm])
                go(g_ref.at[rows, cols], gl.at[at], gs.at[to], gr.at[frm])

        each(1, TILE)
        each(0, TILE // 2)

    def kv_send(i, carry):
        to = lax.rem(me + PEERS - 2 * i, PEERS)
        remote(kvbuf.at[spot(to)[1]], kv_at(me), ks.at[to], kr.at[me], to).start()
        return carry

    lax.fori_loop(1, 8, kv_send, 0)
    remote(kvbuf.at[z], kv_at(me), ks.at[mate], kr.at[me], mate).start()
    own_kv = pltpu.make_async_copy(kvbuf.at[z], kv_at(me), ls.at[0])
    own_kv.start()

    def cnt_send(i, carry):
        to = lax.rem(me + i, PEERS)
        remote(cntbuf, cntall.at[me], cs.at[to], cr.at[me], to).start()
        return carry

    lax.fori_loop(1, PEERS, cnt_send, 0)
    q_copies(me, me, lambda *p: here(*p).start())
    q_copies(mate, me, lambda *p: remote(*p, mate).start())

    whole_core = lax.rem((3 * me + c) // 2, 2)
    shares = ((TILE, whole_core, *piece(me, 1)), (TILE // 2, 1 - whole_core, *piece(me, 0)))

    def q_send(i, carry):
        ch = lax.rem(chip + 8 - i, 8)
        cols = pl.ds(pl.multiple_of(lax.rem(ch, 2) * 512 + (ch // 2) * 128, 128), 128)
        for size, core, src, dst in shares:
            to = 2 * ch + core
            rows = pl.ds(pl.multiple_of(src, 64), size)
            at = pl.ds(pl.multiple_of(dst, 64), size)
            remote(q_ref.at[rows, cols], ql.at[at], qs.at[to], qr.at[me], to).start()
            remote(g_ref.at[rows, cols], gl.at[at], gs.at[to], gr.at[me], to).start()
        return carry

    def kv_pass(i, carry):
        frm = lax.rem(me + 2 * i, PEERS)
        remote(kvbuf.at[0], kv_at(frm), ks.at[frm], kr.at[frm], frm).wait_recv()
        remote(kv_at(frm), kv_at(frm), fs.at[frm], kr.at[frm], mate).start()
        return carry

    lax.fori_loop(1, 8, q_send, 0)
    lax.fori_loop(1, 8, kv_pass, 0)

    def cnt_get(i, carry):
        o = lax.rem(me + i, PEERS)
        cp = remote(cntbuf, cntall.at[o], cs.at[o], cr.at[o], o)
        cp.wait_send()
        cp.wait_recv()
        return carry

    lax.fori_loop(1, PEERS, cnt_get, 0)
    starts = cntall[0, 0]
    ends = cntall[0, 1]
    for i in range(1, PEERS):
        starts = starts + cntall[i, 0]
        ends = ends + cntall[i, 1]
    starts = starts.astype(jnp.int32)
    ends = ends.astype(jnp.int32)
    far = 2 * TOTAL
    q_starts = jnp.where((doc >= 1) & (doc < DOCS), starts, far)
    q_ends = jnp.where(doc < DOCS - 1, ends, far)

    ahead = lax.broadcasted_iota(jnp.int32, (pad, 128), 1) == 0
    docl[:pad] = jnp.where(ahead, 1.0, 0.0).astype(bf16)
    row_256 = lax.broadcasted_iota(jnp.int32, (256, 128), 0)

    def fill(j, carry):
        at = pl.ds(pl.multiple_of(j * 256 + pad, 256), 256)
        docl[at] = jnp.where(row_256 + j * 256 < starts, 1.0, 0.0).astype(bf16)
        return carry

    lax.fori_loop(0, TOTAL // 256, fill, 0)

    def kv_get(i, carry):
        frm = lax.rem(mate + 2 * i, PEERS)
        remote(kvbuf.at[0], kv_at(frm), ks.at[frm], kr.at[frm], frm).wait_recv()
        return carry

    lax.fori_loop(0, 8, kv_get, 0)
    own_kv.wait()

    lane = lax.broadcasted_iota(jnp.int32, (1, LANES), 1)
    sink = jnp.where(lane < TILE, sink_ref[head], sink_ref[head + 1])
    row = lax.broadcasted_iota(jnp.int32, (TILE, 128), 0)
    causal = lax.broadcasted_iota(jnp.int32, (UNIT, LANES), 0) <= (lane & (TILE - 1))
    nt = (((1,), (1,)), ((), ()))
    tn = (((0,), (0,)), ((), ()))

    q_copies(me, me, lambda *p: here(*p).wait())

    def q_wait(frm, size, *_):
        some = pl.ds(0, size)

        @pl.when(frm != me)
        def _():
            remote(q_ref.at[some, :128], ql.at[some], qs.at[frm], qr.at[frm], frm).wait_recv()
            remote(g_ref.at[some, :128], gl.at[some], gs.at[frm], gr.at[frm], frm).wait_recv()

    def dq_copies(to, frm, go):
        fy, fz, fc = spot(frm)
        cols = pl.ds(pl.multiple_of(fz * 512 + fy * 128, 128), 128)

        def each(full, size):
            @pl.when(is_full(to, fc) == full)
            def _():
                dst, src = piece(to, full)
                take = pl.ds(pl.multiple_of(src, 64), size)
                rows = pl.ds(pl.multiple_of(dst, 64), size)
                go(dqb.at[take], dqo_ref.at[rows, cols], ds.at[to], dr.at[frm])

        each(1, TILE)
        each(0, TILE // 2)

    my_cols = pl.ds(pl.multiple_of(z * 512 + y * 128, 128), 128)

    def dq_send(to, size, row, src):
        p = (
            dqb.at[pl.ds(pl.multiple_of(src, 64), size)],
            dqo_ref.at[pl.ds(row, size), my_cols],
            ds.at[to],
            dr.at[me],
        )

        @pl.when(to == me)
        def _():
            here(*p).start()

        @pl.when(to != me)
        def _():
            remote(*p, to).start()

    first_pair = (3 * chip + 3) // 4

    def sources(t, act):
        place = 2 * t + c
        third = lax.rem(place, 3)
        src = 2 * (place // 3)
        n0 = t * TILE

        @pl.when(third == 0)
        def _():
            act(src, TILE, 0, n0)

        @pl.when(third == 1)
        def _():
            act(src, TILE // 2, TILE, n0)
            act(src + 1, TILE // 2, 0, n0 + TILE // 2)

        @pl.when(third == 2)
        def _():
            act(src + 1, TILE, TILE // 2, n0)

    def ready(k, t):
        n0 = pl.multiple_of(t * TILE, TILE)
        p0 = (2 * t + c) * TILE
        qt = (ql[pl.ds(n0, TILE), :].astype(f32) * 0.125).astype(bf16)
        gt = gl[pl.ds(n0, TILE), :]
        none = jnp.zeros((TILE, D), bf16)
        w_ref[k, :TILE] = jnp.concatenate([qt[:, :D], none], axis=1)
        w_ref[k, TILE : 2 * TILE] = jnp.concatenate([qt[:, D:], none], axis=1)
        w_ref[k, 2 * TILE : 3 * TILE] = jnp.concatenate([none, gt[:, :D]], axis=1)
        w_ref[k, 3 * TILE :] = jnp.concatenate([none, gt[:, D:]], axis=1)
        inside = (row + p0 >= q_starts) & (row + p0 < q_ends)
        doc_ref[k] = jnp.where((doc == 0) | inside, FILL, 0.0).astype(bf16)

    def chain(k, t, size):
        wg = w_ref[k, 2 * TILE :]
        docs = jnp.concatenate([doc_ref[k]] * 2, axis=0)
        wq = jnp.concatenate([w_ref[k, : 2 * TILE], docs], axis=1)
        u0 = 2 * t + c + 1 - size + PAD

        def rows(i):
            return pl.ds(pl.multiple_of((u0 + i) * UNIT, UNIT), SUB * UNIT)

        subs = list(range(0, size, SUB))[::-1]
        top = sink
        mass = jnp.zeros((8, LANES), f32)
        tops = {}
        for i in subs:
            kv = kvl[rows(i), :]
            at = slice(i * UNIT, (i + SUB) * UNIT)
            kvd = jnp.concatenate([kv, docl[rows(i), :]], axis=1)
            s = lax.dot_general(kvd, wq, nt, preferred_element_type=f32)
            dp_ref[k, at, :] = lax.dot_general(kv, wg, nt, preferred_element_type=f32)
            if i + SUB == size:
                s = jnp.concatenate([s[:-UNIT], jnp.where(causal, s[-UNIT:], FILL)], axis=0)
            new = jnp.maximum(top, jnp.max(fold(s, jnp.max), axis=0, keepdims=True))
            e = jnp.exp2((s - new) * LOG2E)
            s_ref[k, at, :] = e
            mass = mass * jnp.exp2((top - new) * LOG2E) + fold(e, jnp.sum)
            top = tops[i] = new
            yield
        sink_e = jnp.exp2((sink - top) * LOG2E)
        inv = 1.0 / (jnp.sum(mass, axis=0, keepdims=True) + sink_e)

        delta = jnp.zeros((8, LANES), f32)
        scale = {}
        for i in subs:
            at = slice(i * UNIT, (i + SUB) * UNIT)
            scale[i] = jnp.exp2((tops[i] - top) * LOG2E) * inv
            prob_half = (s_ref[k, at, :] * scale[i]).astype(bf16).astype(f32)
            delta = delta + fold(prob_half * dp_ref[k, at, :], jnp.sum)
            yield
        delta = jnp.sum(delta, axis=0, keepdims=True)
        gacc_ref[...] += sink_e * inv * delta

        dq = jnp.zeros((LANES, 128), f32)
        w = w_ref[k]
        for i in subs:
            at = slice(i * UNIT, (i + SUB) * UNIT)
            prob = s_ref[k, at, :] * scale[i]
            dscore = (prob * (dp_ref[k, at, :] - delta)).astype(bf16)
            x = jnp.concatenate([dscore, prob.astype(bf16)], axis=1)
            acc_ref[rows(i), :] += jnp.dot(x, w, preferred_element_type=f32)
            dq = dq + lax.dot_general(dscore, kvl[rows(i), :], tn, preferred_element_type=f32)
            yield
        dq = dq[:, :D] * 0.125
        dq = jnp.concatenate([dq[:TILE], dq[TILE:]], axis=1)
        dqb[pl.ds(pl.multiple_of(t * TILE, TILE), TILE), :] = dq.astype(bf16)

    def pair(i, carry):
        p = lax.rem(first_pair + i, TILES // 2)
        for k in range(2):
            sources(2 * p + k, q_wait)
            ready(k, 2 * p + k)

        def run(n):
            left = [chain(k, 2 * p + k, min(4 * n + 2 * k + 2, LONGEST)) for k in range(2)]
            while left:
                left = [steps for steps in left if next(steps, 0) is None]

        for n in range(TILES // 2):
            pl.when(p == n)(functools.partial(run, n))
        for k in range(2):
            sources(2 * p + k, dq_send)
        return carry

    lax.fori_loop(0, TILES // 2, pair, 0)

    g = gacc_ref[...]
    ga = -jnp.sum(g[:, :TILE], axis=1, keepdims=True)
    gb = -jnp.sum(g[:, TILE:], axis=1, keepdims=True)
    gbuf[0] = jnp.where(doc == head, ga, jnp.where(doc == head + 1, gb, 0.0))
    g_mate = remote(gbuf.at[0], gbuf.at[1], es.at[8], er.at[8], mate)
    g_mate.start()

    def block(b, core):
        return pl.ds(pl.multiple_of((2 * b + core) * ROWS + pad, 64), ROWS)

    def mate_send(i, carry):
        b = lax.rem(2 * y + z + 8 - i, 8)
        half[b] = acc_ref[block(b, 1 - c), :].astype(bf16)
        remote(half.at[b], mine.at[b], ms.at[b], mr.at[b], mate).start()
        return carry

    lax.fori_loop(1, 9, mate_send, 0)

    def chip_sum(b):
        remote(half.at[b], mine.at[b], ms.at[b], mr.at[b], mate).wait_recv()
        return (acc_ref[block(b, c), :] + mine[b].astype(f32)).astype(bf16)

    def sum_send(i, carry):
        b = lax.rem(2 * y + z + 8 - i, 8)
        sums[b] = chip_sum(b)
        to = 2 * b + c
        remote(sums.at[b], land.at[2 * y + z], ss.at[b], sr.at[2 * y + z], to).start()
        return carry

    lax.fori_loop(1, 8, sum_send, 0)
    land[2 * y + z] = chip_sum(2 * y + z)

    g_mate.wait()
    gbuf[2] = gbuf[0] + gbuf[1]
    gall[chip] = gbuf[2]

    def g_send(i, carry):
        ch = lax.rem(chip + i, 8)
        remote(gbuf.at[2], gall.at[chip], es.at[ch], er.at[chip], 2 * ch + c).start()
        return carry

    lax.fori_loop(1, 8, g_send, 0)

    def kv_sent(i, carry):
        to = lax.rem(me + 2 * i, PEERS)
        remote(kvbuf.at[0], kv_at(me), ks.at[to], kr.at[me], to).wait_send()
        remote(kv_at(to), kv_at(to), fs.at[to], kr.at[to], mate).wait_send()
        return carry

    lax.fori_loop(1, 8, kv_sent, 0)
    remote(kvbuf.at[0], kv_at(me), ks.at[mate], kr.at[me], mate).wait_send()

    def mate_sent(b, carry):
        remote(half.at[b], mine.at[b], ms.at[b], mr.at[b], mate).wait_send()
        return carry

    lax.fori_loop(0, 8, mate_sent, 0)

    def dq_sent(ch, size):
        some = pl.ds(0, size)
        for core in range(2):
            to = 2 * ch + core
            remote(dqb.at[some], dqo_ref.at[some, my_cols], ds.at[to], dr.at[to], to).wait_send()

    def rest(i, carry):
        ch = lax.rem(chip + i, 8)
        for size, core, _, _ in shares:
            o = 2 * ch + core
            some = pl.ds(0, size)
            remote(q_ref.at[some, :128], ql.at[some], qs.at[o], qr.at[o], o).wait_send()
            remote(g_ref.at[some, :128], gl.at[some], gs.at[o], gr.at[o], o).wait_send()
            remote(dqb.at[some], dqo_ref.at[some, my_cols], ds.at[o], dr.at[o], o).wait_recv()
        pl.when(lax.rem(ch + c, 2) == 0)(lambda: dq_sent(ch, TILE))
        pl.when(lax.rem(ch + c, 2) == 1)(lambda: dq_sent(ch, TILE // 2))
        cp = remote(gbuf.at[2], gall.at[ch], es.at[ch], er.at[ch], 2 * ch + c)
        cp.wait_send()
        cp.wait_recv()
        return carry

    lax.fori_loop(1, 8, rest, 0)
    q_copies(mate, me, lambda *p: remote(*p, mate).wait_send())
    dq_copies(mate, me, lambda *p: remote(*p, mate).wait_send())
    dq_copies(me, mate, lambda *p: remote(*p, mate).wait_recv())
    dq_copies(me, me, lambda *p: here(*p).wait())
    total = gall[0]
    for i in range(1, 8):
        total = total + gall[i]
    gso_ref[...] = total[0, :16]

    def sum_get(i, carry):
        b = lax.rem(2 * y + z + i, 8)
        cp = remote(sums.at[b], land.at[b], ss.at[b], sr.at[b], 2 * b + c)
        cp.wait_send()
        cp.wait_recv()
        return carry

    lax.fori_loop(1, 8, sum_get, 0)
    heads = []
    for h in range(2):
        heads.append(
            (land[h].astype(f32) + land[2 + h].astype(f32))
            + (land[4 + h].astype(f32) + land[6 + h].astype(f32))
        )
    dk_ref[...] = jnp.concatenate([heads[0][:, :D], heads[1][:, :D]], axis=1).astype(bf16)
    dv_ref[...] = jnp.concatenate([heads[0][:, D:], heads[1][:, D:]], axis=1).astype(bf16)


def whole(q, g, k, v, seg, sinks):
    hbm = pl.BlockSpec(memory_space=pltpu.HBM)
    vmem = pl.BlockSpec(memory_space=pltpu.VMEM)
    sem = pltpu.SemaphoreType.DMA
    blocks = pltpu.VMEM((8, ROWS, 128), bf16)
    longest = LONGEST * UNIT
    return pl.pallas_call(
        whole_kernel,
        name="whole",
        out_shape=(
            jax.ShapeDtypeStruct((ROWS, 1024), bf16),
            jax.ShapeDtypeStruct((ROWS, 128), bf16),
            jax.ShapeDtypeStruct((ROWS, 128), bf16),
            jax.ShapeDtypeStruct((16,), f32),
        ),
        in_specs=[hbm] * 6,
        out_specs=(hbm, vmem, vmem, vmem),
        scratch_shapes=[
            pltpu.VMEM((ROWS, 128), bf16),
            pltpu.VMEM((ROWS, 128), bf16),
            pltpu.VMEM((1, ROWS), jnp.int32),
            pltpu.SMEM((16,), f32),
            pltpu.VMEM((2, ROWS, 128), bf16),
            pltpu.VMEM((2, 1, 128), f32),
            pltpu.VMEM((PEERS, 2, 1, 128), f32),
            pltpu.VMEM((TOTAL // 2, 128), bf16),
            pltpu.VMEM((TOTAL // 2, 128), bf16),
            pltpu.VMEM((PADDED, 128), bf16),
            pltpu.VMEM((PADDED, 128), bf16),
            pltpu.VMEM((PADDED, 128), f32),
            pltpu.VMEM((2, longest, LANES), f32),
            pltpu.VMEM((2, longest, LANES), f32),
            pltpu.VMEM((1, LANES), f32),
            pltpu.VMEM((2, 4 * TILE, 128), bf16),
            pltpu.VMEM((2, TILE, 128), bf16),
            pltpu.VMEM((TOTAL // 2, 128), bf16),
            blocks,
            blocks,
            blocks,
            blocks,
            pltpu.VMEM((3, 1, 128), f32),
            pltpu.VMEM((8, 1, 128), f32),
        ]
        + [sem((PEERS,))] * 13
        + [sem((8,))] * 4
        + [sem((5,))],
        compiler_params=pltpu.CompilerParams(
            collective_id=0, has_side_effects=True, vmem_limit_bytes=GRANT
        ),
    )(q, g, k, v, seg, sinks)


def hand_over_kernel(*refs):
    sems = refs[-2:]
    n = (len(refs) - 2) // 3
    moves = []
    for i in range(n):
        src, dst, via = refs[i], refs[n + i], refs[2 * n + i]
        parts = [pl.ds(r, 48) for r in range(0, ROWS, 48)] if src.shape[1:] == (1024,) else [None]
        for part in parts:
            ref = [r if part is None else r.at[part] for r in (src, via, dst)]
            k = len(moves)
            moves.append(
                (
                    pltpu.make_async_copy(ref[0], ref[1], sems[0].at[k]),
                    pltpu.make_async_copy(ref[1], ref[2], sems[1].at[k]),
                )
            )
    for come, _ in moves:
        come.start()
    for come, go in moves:
        come.wait()
        go.start()
    for _, go in moves:
        go.wait()


def hand_over(*arrays):
    hbm = pl.BlockSpec(memory_space=pltpu.HBM)
    shapes = [(a.shape, a.dtype) for a in arrays]
    return pl.pallas_call(
        hand_over_kernel,
        name="hand_over",
        out_shape=tuple(jax.ShapeDtypeStruct(*a) for a in shapes),
        in_specs=[hbm] * len(arrays),
        out_specs=(hbm,) * len(arrays),
        scratch_shapes=[pltpu.VMEM(*a) for a in shapes]
        + [pltpu.SemaphoreType.DMA((16,))] * 2,
        compiler_params=pltpu.CompilerParams(vmem_limit_bytes=GRANT),
    )(*arrays)


def on_device(queries, keys, values, grad_out, segments, sinks):
    grad_q, dk, dv, grad_sinks = whole(
        queries, grad_out, keys, values, segments.reshape(1, ROWS), sinks
    )
    return hand_over(grad_q, dk, dv, grad_sinks)


def solution(mesh):
    rows = P(("dp", "ctx"), "tp")
    return jax.shard_map(
        on_device,
        mesh=mesh,
        in_specs=(rows, rows, rows, rows, P(("dp", "ctx")), P("tp")),
        out_specs=(rows, rows, rows, P(("dp", "tp"))),
        check_vma=False,
    )
```

```python
import functools

import jax
import jax.numpy as jnp
from jax import lax
from jax.experimental import pallas as pl
from jax.experimental.pallas import tpu as pltpu
from jax.sharding import PartitionSpec as P

D = 64
PEERS = 16
ROWS = 192
TOTAL = PEERS * ROWS
DOCS = 6
TILE = 128
TILES = TOTAL // TILE // 2
LANES = 2 * TILE
UNIT = 128
SUB = 2
PAD = 4
PADDED = TOTAL + PAD * UNIT
LONGEST = 20
GRANT = 63 * 1024 * 1024
LOG2E = 1.4426950408889634
FILL = -1e30
f32 = jnp.float32
bf16 = jnp.bfloat16


def spot(i):
    return i // 4, lax.rem(i // 2, 2), lax.rem(i, 2)


def is_full(block, core):
    tile = (3 * block + lax.rem(block, 2)) // 2
    return 1 - lax.rem(tile + core, 2)


def piece(block, full):
    odd = lax.rem(block, 2)
    first = odd if full else 2 - 2 * odd
    g = 3 * block + first
    return 64 * first, (g // 4) * TILE + lax.rem(g, 2) * 64


def remote(src, dst, send, recv, to):
    return pltpu.make_async_remote_copy(
        src_ref=src,
        dst_ref=dst,
        send_sem=send,
        recv_sem=recv,
        device_id={"ctx": to},
        device_id_type=pl.DeviceIdType.MESH,
    )


def here(src, dst, _, sem):
    return pltpu.make_async_copy(src, dst, sem)


def greet(me):
    def hello(i, carry):
        to = lax.rem(me + i, PEERS)
        pl.semaphore_signal(
            pltpu.get_barrier_semaphore(),
            inc=1,
            device_id={"ctx": to},
            device_id_type=pl.DeviceIdType.MESH,
        )
        return carry

    lax.fori_loop(1, PEERS, hello, 0)


def fold(x, op):
    return op(x.reshape(x.shape[0] // 8, 8, LANES), axis=0)


def whole_kernel(
    q_ref, g_ref, k_hbm, v_hbm, seg_hbm, sink_hbm,
    dqo_ref, dk_ref, dv_ref, gso_ref,
    k_ref, v_ref, seg_ref, sink_ref, kvbuf, cntbuf, cntall, ql, gl, kvl, docl, acc_ref, s_ref, dp_ref, gacc_ref, w_ref, doc_ref,
    dqb, half, mine, sums, land, gbuf, gall,
    ks, kr, fs, cs, cr, qs, qr, gs, gr, ds, dr, es, er, ms, mr, ss, sr, ls,
):
    me = lax.axis_index("ctx")
    y, z, c = spot(me)
    chip = me // 2
    mate = me + 1 - 2 * c
    head = 8 * z + 2 * y
    pad = PAD * UNIT

    greet(me)
    fetch = [
        pltpu.make_async_copy(src, dst, ls.at[1 + i])
        for i, (src, dst) in enumerate(
            [(k_hbm, k_ref), (v_hbm, v_ref), (seg_hbm, seg_ref), (sink_hbm, sink_ref)]
        )
    ]
    for f in fetch:
        f.start()
    acc_ref[...] = jnp.zeros_like(acc_ref)
    gacc_ref[...] = jnp.zeros_like(gacc_ref)
    kvl[:pad] = jnp.zeros((pad, 128), bf16)
    for f in fetch:
        f.wait()

    for h in range(2):
        kvbuf[h] = jnp.concatenate(
            [k_ref[:, h * D : (h + 1) * D], v_ref[:, h * D : (h + 1) * D]], axis=1
        )
    doc = lax.broadcasted_iota(jnp.int32, (1, 128), 1)
    counts = [jnp.zeros((1, 128), f32), jnp.zeros((1, 128), f32)]
    for d in range(1, DOCS):
        below = jnp.sum(jnp.where(seg_ref[...] < d, 1.0, 0.0), axis=1, keepdims=True)
        counts[0] = jnp.where(doc == d, below, counts[0])
        counts[1] = jnp.where(doc == d - 1, below, counts[1])
    for i in range(2):
        cntbuf[i] = counts[i]
        cntall[me, i] = counts[i]

    pl.semaphore_wait(pltpu.get_barrier_semaphore(), PEERS - 1)

    def kv_at(i):
        return kvl.at[pl.ds(pl.multiple_of(i * ROWS + pad, 64), ROWS)]

    def q_copies(to, frm, go):
        ty, tz, tc = spot(to)
        cols = pl.ds(pl.multiple_of(tz * 512 + ty * 128, 128), 128)

        def each(full, size):
            @pl.when(is_full(frm, tc) == full)
            def _():
                src, dst = piece(frm, full)
                rows = pl.ds(pl.multiple_of(src, 64), size)
                at = pl.ds(pl.multiple_of(dst, 64), size)
                go(q_ref.at[rows, cols], ql.at[at], qs.at[to], qr.at[frm])
                go(g_ref.at[rows, cols], gl.at[at], gs.at[to], gr.at[frm])

        each(1, TILE)
        each(0, TILE // 2)

    def kv_send(i, carry):
        to = lax.rem(me + PEERS - 2 * i, PEERS)
        remote(kvbuf.at[spot(to)[1]], kv_at(me), ks.at[to], kr.at[me], to).start()
        return carry

    lax.fori_loop(1, 8, kv_send, 0)
    remote(kvbuf.at[z], kv_at(me), ks.at[mate], kr.at[me], mate).start()
    own_kv = pltpu.make_async_copy(kvbuf.at[z], kv_at(me), ls.at[0])
    own_kv.start()

    def cnt_send(i, carry):
        to = lax.rem(me + i, PEERS)
        remote(cntbuf, cntall.at[me], cs.at[to], cr.at[me], to).start()
        return carry

    lax.fori_loop(1, PEERS, cnt_send, 0)
    q_copies(me, me, lambda *p: here(*p).start())
    q_copies(mate, me, lambda *p: remote(*p, mate).start())

    whole_core = lax.rem((3 * me + c) // 2, 2)
    shares = ((TILE, whole_core, *piece(me, 1)), (TILE // 2, 1 - whole_core, *piece(me, 0)))

    def q_send(i, carry):
        ch = lax.rem(chip + 8 - i, 8)
        cols = pl.ds(pl.multiple_of(lax.rem(ch, 2) * 512 + (ch // 2) * 128, 128), 128)
        for size, core, src, dst in shares:
            to = 2 * ch + core
            rows = pl.ds(pl.multiple_of(src, 64), size)
            at = pl.ds(pl.multiple_of(dst, 64), size)
            remote(q_ref.at[rows, cols], ql.at[at], qs.at[to], qr.at[me], to).start()
            remote(g_ref.at[rows, cols], gl.at[at], gs.at[to], gr.at[me], to).start()
        return carry

    def kv_pass(i, carry):
        frm = lax.rem(me + 2 * i, PEERS)
        remote(kvbuf.at[0], kv_at(frm), ks.at[frm], kr.at[frm], frm).wait_recv()
        remote(kv_at(frm), kv_at(frm), fs.at[frm], kr.at[frm], mate).start()
        return carry

    lax.fori_loop(1, 8, q_send, 0)
    lax.fori_loop(1, 8, kv_pass, 0)

    def cnt_get(i, carry):
        o = lax.rem(me + i, PEERS)
        cp = remote(cntbuf, cntall.at[o], cs.at[o], cr.at[o], o)
        cp.wait_send()
        cp.wait_recv()
        return carry

    lax.fori_loop(1, PEERS, cnt_get, 0)
    starts = cntall[0, 0]
    ends = cntall[0, 1]
    for i in range(1, PEERS):
        starts = starts + cntall[i, 0]
        ends = ends + cntall[i, 1]
    starts = starts.astype(jnp.int32)
    ends = ends.astype(jnp.int32)
    far = 2 * TOTAL
    q_starts = jnp.where((doc >= 1) & (doc < DOCS), starts, far)
    q_ends = jnp.where(doc < DOCS - 1, ends, far)

    ahead = lax.broadcasted_iota(jnp.int32, (pad, 128), 1) == 0
    docl[:pad] = jnp.where(ahead, 1.0, 0.0).astype(bf16)
    row_256 = lax.broadcasted_iota(jnp.int32, (256, 128), 0)

    def fill(j, carry):
        at = pl.ds(pl.multiple_of(j * 256 + pad, 256), 256)
        docl[at] = jnp.where(row_256 + j * 256 < starts, 1.0, 0.0).astype(bf16)
        return carry

    lax.fori_loop(0, TOTAL // 256, fill, 0)

    def kv_get(i, carry):
        frm = lax.rem(mate + 2 * i, PEERS)
        remote(kvbuf.at[0], kv_at(frm), ks.at[frm], kr.at[frm], frm).wait_recv()
        return carry

    lax.fori_loop(0, 8, kv_get, 0)
    own_kv.wait()

    lane = lax.broadcasted_iota(jnp.int32, (1, LANES), 1)
    sink = jnp.where(lane < TILE, sink_ref[head], sink_ref[head + 1])
    row = lax.broadcasted_iota(jnp.int32, (TILE, 128), 0)
    causal = lax.broadcasted_iota(jnp.int32, (UNIT, LANES), 0) <= (lane & (TILE - 1))
    nt = (((1,), (1,)), ((), ()))
    tn = (((0,), (0,)), ((), ()))

    q_copies(me, me, lambda *p: here(*p).wait())

    def q_wait(frm, size, *_):
        some = pl.ds(0, size)

        @pl.when(frm != me)
        def _():
            remote(q_ref.at[some, :128], ql.at[some], qs.at[frm], qr.at[frm], frm).wait_recv()
            remote(g_ref.at[some, :128], gl.at[some], gs.at[frm], gr.at[frm], frm).wait_recv()

    def dq_copies(to, frm, go):
        fy, fz, fc = spot(frm)
        cols = pl.ds(pl.multiple_of(fz * 512 + fy * 128, 128), 128)

        def each(full, size):
            @pl.when(is_full(to, fc) == full)
            def _():
                dst, src = piece(to, full)
                take = pl.ds(pl.multiple_of(src, 64), size)
                rows = pl.ds(pl.multiple_of(dst, 64), size)
                go(dqb.at[take], dqo_ref.at[rows, cols], ds.at[to], dr.at[frm])

        each(1, TILE)
        each(0, TILE // 2)

    my_cols = pl.ds(pl.multiple_of(z * 512 + y * 128, 128), 128)

    def dq_send(to, size, row, src):
        p = (
            dqb.at[pl.ds(pl.multiple_of(src, 64), size)],
            dqo_ref.at[pl.ds(row, size), my_cols],
            ds.at[to],
            dr.at[me],
        )

        @pl.when(to == me)
        def _():
            here(*p).start()

        @pl.when(to != me)
        def _():
            remote(*p, to).start()

    first_pair = (3 * chip + 3) // 4

    def sources(t, act):
        place = 2 * t + c
        third = lax.rem(place, 3)
        src = 2 * (place // 3)
        n0 = t * TILE

        @pl.when(third == 0)
        def _():
            act(src, TILE, 0, n0)

        @pl.when(third == 1)
        def _():
            act(src, TILE // 2, TILE, n0)
            act(src + 1, TILE // 2, 0, n0 + TILE // 2)

        @pl.when(third == 2)
        def _():
            act(src + 1, TILE, TILE // 2, n0)

    def ready(k, t):
        n0 = pl.multiple_of(t * TILE, TILE)
        p0 = (2 * t + c) * TILE
        qt = (ql[pl.ds(n0, TILE), :].astype(f32) * 0.125).astype(bf16)
        gt = gl[pl.ds(n0, TILE), :]
        none = jnp.zeros((TILE, D), bf16)
        w_ref[k, :TILE] = jnp.concatenate([qt[:, :D], none], axis=1)
        w_ref[k, TILE : 2 * TILE] = jnp.concatenate([qt[:, D:], none], axis=1)
        w_ref[k, 2 * TILE : 3 * TILE] = jnp.concatenate([none, gt[:, :D]], axis=1)
        w_ref[k, 3 * TILE :] = jnp.concatenate([none, gt[:, D:]], axis=1)
        inside = (row + p0 >= q_starts) & (row + p0 < q_ends)
        doc_ref[k] = jnp.where((doc == 0) | inside, FILL, 0.0).astype(bf16)

    def chain(k, t, size):
        wg = w_ref[k, 2 * TILE :]
        docs = jnp.concatenate([doc_ref[k]] * 2, axis=0)
        wq = jnp.concatenate([w_ref[k, : 2 * TILE], docs], axis=1)
        u0 = 2 * t + c + 1 - size + PAD

        def rows(i):
            return pl.ds(pl.multiple_of((u0 + i) * UNIT, UNIT), SUB * UNIT)

        subs = list(range(0, size, SUB))[::-1]
        top = sink
        mass = jnp.zeros((8, LANES), f32)
        tops = {}
        for i in subs:
            kv = kvl[rows(i), :]
            at = slice(i * UNIT, (i + SUB) * UNIT)
            kvd = jnp.concatenate([kv, docl[rows(i), :]], axis=1)
            s = lax.dot_general(kvd, wq, nt, preferred_element_type=f32)
            dp_ref[k, at, :] = lax.dot_general(kv, wg, nt, preferred_element_type=f32)
            if i + SUB == size:
                s = jnp.concatenate([s[:-UNIT], jnp.where(causal, s[-UNIT:], FILL)], axis=0)
            new = jnp.maximum(top, jnp.max(fold(s, jnp.max), axis=0, keepdims=True))
            e = jnp.exp2((s - new) * LOG2E)
            s_ref[k, at, :] = e
            mass = mass * jnp.exp2((top - new) * LOG2E) + fold(e, jnp.sum)
            top = tops[i] = new
            yield
        sink_e = jnp.exp2((sink - top) * LOG2E)
        inv = 1.0 / (jnp.sum(mass, axis=0, keepdims=True) + sink_e)

        delta = jnp.zeros((8, LANES), f32)
        scale = {}
        for i in subs:
            at = slice(i * UNIT, (i + SUB) * UNIT)
            scale[i] = jnp.exp2((tops[i] - top) * LOG2E) * inv
            prob_half = (s_ref[k, at, :] * scale[i]).astype(bf16).astype(f32)
            delta = delta + fold(prob_half * dp_ref[k, at, :], jnp.sum)
            yield
        delta = jnp.sum(delta, axis=0, keepdims=True)
        gacc_ref[...] += sink_e * inv * delta

        dq = jnp.zeros((LANES, 128), f32)
        w = w_ref[k]
        for i in subs:
            at = slice(i * UNIT, (i + SUB) * UNIT)
            prob = s_ref[k, at, :] * scale[i]
            dscore = (prob * (dp_ref[k, at, :] - delta)).astype(bf16)
            x = jnp.concatenate([dscore, prob.astype(bf16)], axis=1)
            acc_ref[rows(i), :] += jnp.dot(x, w, preferred_element_type=f32)
            dq = dq + lax.dot_general(dscore, kvl[rows(i), :], tn, preferred_element_type=f32)
            yield
        dq = dq[:, :D] * 0.125
        dq = jnp.concatenate([dq[:TILE], dq[TILE:]], axis=1)
        dqb[pl.ds(pl.multiple_of(t * TILE, TILE), TILE), :] = dq.astype(bf16)

    def pair(i, carry):
        p = lax.rem(first_pair + i, TILES // 2)
        for k in range(2):
            sources(2 * p + k, q_wait)
            ready(k, 2 * p + k)

        def run(n):
            left = [chain(k, 2 * p + k, min(4 * n + 2 * k + 2, LONGEST)) for k in range(2)]
            while left:
                left = [steps for steps in left if next(steps, 0) is None]

        for n in range(TILES // 2):
            pl.when(p == n)(functools.partial(run, n))
        for k in range(2):
            sources(2 * p + k, dq_send)
        return carry

    lax.fori_loop(0, TILES // 2, pair, 0)

    g = gacc_ref[...]
    ga = -jnp.sum(g[:, :TILE], axis=1, keepdims=True)
    gb = -jnp.sum(g[:, TILE:], axis=1, keepdims=True)
    gbuf[0] = jnp.where(doc == head, ga, jnp.where(doc == head + 1, gb, 0.0))
    g_mate = remote(gbuf.at[0], gbuf.at[1], es.at[8], er.at[8], mate)
    g_mate.start()

    def block(b, core):
        return pl.ds(pl.multiple_of((2 * b + core) * ROWS + pad, 64), ROWS)

    def mate_send(i, carry):
        b = lax.rem(2 * y + z + 8 - i, 8)
        half[b] = acc_ref[block(b, 1 - c), :].astype(bf16)
        remote(half.at[b], mine.at[b], ms.at[b], mr.at[b], mate).start()
        return carry

    lax.fori_loop(1, 9, mate_send, 0)

    def chip_sum(b):
        remote(half.at[b], mine.at[b], ms.at[b], mr.at[b], mate).wait_recv()
        return (acc_ref[block(b, c), :] + mine[b].astype(f32)).astype(bf16)

    def sum_send(i, carry):
        b = lax.rem(2 * y + z + 8 - i, 8)
        sums[b] = chip_sum(b)
        to = 2 * b + c
        remote(sums.at[b], land.at[2 * y + z], ss.at[b], sr.at[2 * y + z], to).start()
        return carry

    lax.fori_loop(1, 8, sum_send, 0)
    land[2 * y + z] = chip_sum(2 * y + z)

    g_mate.wait()
    gbuf[2] = gbuf[0] + gbuf[1]
    gall[chip] = gbuf[2]

    def g_send(i, carry):
        ch = lax.rem(chip + i, 8)
        remote(gbuf.at[2], gall.at[chip], es.at[ch], er.at[chip], 2 * ch + c).start()
        return carry

    lax.fori_loop(1, 8, g_send, 0)

    def kv_sent(i, carry):
        to = lax.rem(me + 2 * i, PEERS)
        remote(kvbuf.at[0], kv_at(me), ks.at[to], kr.at[me], to).wait_send()
        remote(kv_at(to), kv_at(to), fs.at[to], kr.at[to], mate).wait_send()
        return carry

    lax.fori_loop(1, 8, kv_sent, 0)
    remote(kvbuf.at[0], kv_at(me), ks.at[mate], kr.at[me], mate).wait_send()

    def mate_sent(b, carry):
        remote(half.at[b], mine.at[b], ms.at[b], mr.at[b], mate).wait_send()
        return carry

    lax.fori_loop(0, 8, mate_sent, 0)

    def dq_sent(ch, size):
        some = pl.ds(0, size)
        for core in range(2):
            to = 2 * ch + core
            remote(dqb.at[some], dqo_ref.at[some, my_cols], ds.at[to], dr.at[to], to).wait_send()

    def rest(i, carry):
        ch = lax.rem(chip + i, 8)
        for size, core, _, _ in shares:
            o = 2 * ch + core
            some = pl.ds(0, size)
            remote(q_ref.at[some, :128], ql.at[some], qs.at[o], qr.at[o], o).wait_send()
            remote(g_ref.at[some, :128], gl.at[some], gs.at[o], gr.at[o], o).wait_send()
            remote(dqb.at[some], dqo_ref.at[some, my_cols], ds.at[o], dr.at[o], o).wait_recv()
        pl.when(lax.rem(ch + c, 2) == 0)(lambda: dq_sent(ch, TILE))
        pl.when(lax.rem(ch + c, 2) == 1)(lambda: dq_sent(ch, TILE // 2))
        cp = remote(gbuf.at[2], gall.at[ch], es.at[ch], er.at[ch], 2 * ch + c)
        cp.wait_send()
        cp.wait_recv()
        return carry

    lax.fori_loop(1, 8, rest, 0)
    q_copies(mate, me, lambda *p: remote(*p, mate).wait_send())
    dq_copies(mate, me, lambda *p: remote(*p, mate).wait_send())
    dq_copies(me, mate, lambda *p: remote(*p, mate).wait_recv())
    dq_copies(me, me, lambda *p: here(*p).wait())
    total = gall[0]
    for i in range(1, 8):
        total = total + gall[i]
    gso_ref[...] = total[0, :16]

    def sum_get(i, carry):
        b = lax.rem(2 * y + z + i, 8)
        cp = remote(sums.at[b], land.at[b], ss.at[b], sr.at[b], 2 * b + c)
        cp.wait_send()
        cp.wait_recv()
        return carry

    lax.fori_loop(1, 8, sum_get, 0)
    heads = []
    for h in range(2):
        heads.append(
            (land[h].astype(f32) + land[2 + h].astype(f32))
            + (land[4 + h].astype(f32) + land[6 + h].astype(f32))
        )
    dk_ref[...] = jnp.concatenate([heads[0][:, :D], heads[1][:, :D]], axis=1).astype(bf16)
    dv_ref[...] = jnp.concatenate([heads[0][:, D:], heads[1][:, D:]], axis=1).astype(bf16)


def whole(q, g, k, v, seg, sinks):
    hbm = pl.BlockSpec(memory_space=pltpu.HBM)
    vmem = pl.BlockSpec(memory_space=pltpu.VMEM)
    sem = pltpu.SemaphoreType.DMA
    blocks = pltpu.VMEM((8, ROWS, 128), bf16)
    longest = LONGEST * UNIT
    return pl.pallas_call(
        whole_kernel,
        name="whole",
        out_shape=(
            jax.ShapeDtypeStruct((ROWS, 1024), bf16),
            jax.ShapeDtypeStruct((ROWS, 128), bf16),
            jax.ShapeDtypeStruct((ROWS, 128), bf16),
            jax.ShapeDtypeStruct((16,), f32),
        ),
        in_specs=[hbm] * 6,
        out_specs=(hbm, vmem, vmem, vmem),
        scratch_shapes=[
            pltpu.VMEM((ROWS, 128), bf16),
            pltpu.VMEM((ROWS, 128), bf16),
            pltpu.VMEM((1, ROWS), jnp.int32),
            pltpu.SMEM((16,), f32),
            pltpu.VMEM((2, ROWS, 128), bf16),
            pltpu.VMEM((2, 1, 128), f32),
            pltpu.VMEM((PEERS, 2, 1, 128), f32),
            pltpu.VMEM((TOTAL // 2, 128), bf16),
            pltpu.VMEM((TOTAL // 2, 128), bf16),
            pltpu.VMEM((PADDED, 128), bf16),
            pltpu.VMEM((PADDED, 128), bf16),
            pltpu.VMEM((PADDED, 128), f32),
            pltpu.VMEM((2, longest, LANES), f32),
            pltpu.VMEM((2, longest, LANES), f32),
            pltpu.VMEM((1, LANES), f32),
            pltpu.VMEM((2, 4 * TILE, 128), bf16),
            pltpu.VMEM((2, TILE, 128), bf16),
            pltpu.VMEM((TOTAL // 2, 128), bf16),
            blocks,
            blocks,
            blocks,
            blocks,
            pltpu.VMEM((3, 1, 128), f32),
            pltpu.VMEM((8, 1, 128), f32),
        ]
        + [sem((PEERS,))] * 13
        + [sem((8,))] * 4
        + [sem((5,))],
        compiler_params=pltpu.CompilerParams(
            collective_id=0, has_side_effects=True, vmem_limit_bytes=GRANT
        ),
    )(q, g, k, v, seg, sinks)


def hand_over_kernel(*refs):
    sems = refs[-2:]
    n = (len(refs) - 2) // 3
    moves = []
    for i in range(n):
        src, dst, via = refs[i], refs[n + i], refs[2 * n + i]
        parts = [pl.ds(r, 16) for r in range(0, ROWS, 16)] if src.shape[1:] == (1024,) else [None]
        for part in parts:
            ref = [r if part is None else r.at[part] for r in (src, via, dst)]
            k = len(moves)
            moves.append(
                (
                    pltpu.make_async_copy(ref[0], ref[1], sems[0].at[k]),
                    pltpu.make_async_copy(ref[1], ref[2], sems[1].at[k]),
                )
            )
    for come, _ in moves:
        come.start()
    for come, go in moves:
        come.wait()
        go.start()
    for _, go in moves:
        go.wait()


def hand_over(*arrays):
    hbm = pl.BlockSpec(memory_space=pltpu.HBM)
    shapes = [(a.shape, a.dtype) for a in arrays]
    return pl.pallas_call(
        hand_over_kernel,
        name="hand_over",
        out_shape=tuple(jax.ShapeDtypeStruct(*a) for a in shapes),
        in_specs=[hbm] * len(arrays),
        out_specs=(hbm,) * len(arrays),
        scratch_shapes=[pltpu.VMEM(*a) for a in shapes]
        + [pltpu.SemaphoreType.DMA((16,))] * 2,
        compiler_params=pltpu.CompilerParams(vmem_limit_bytes=GRANT),
    )(*arrays)


def on_device(queries, keys, values, grad_out, segments, sinks):
    grad_q, dk, dv, grad_sinks = whole(
        queries, grad_out, keys, values, segments.reshape(1, ROWS), sinks
    )
    return hand_over(grad_q, dk, dv, grad_sinks)


def solution(mesh):
    rows = P(("dp", "ctx"), "tp")
    return jax.shard_map(
        on_device,
        mesh=mesh,
        in_specs=(rows, rows, rows, rows, P(("dp", "ctx")), P("tp")),
        out_specs=(rows, rows, rows, P(("dp", "tp"))),
        check_vma=False,
    )
```
